768 devices in a mesh: px: 96 (over z, y_hi, x), py: 8 (over y_lo, core).
Axes of the slice: x: 4, y: 8 (y_hi: 2, y_lo: 4; y = y_hi * 4 + y_lo), z: 12, core: 2. Of those that a mesh axis runs over, the one named last changes fastest.
Arguments:
- displacement: float32 [3, 384, 128, 128], P(None, 'px', 'py'), may hold values from -6 to 6
- velocity: float32 [3, 384, 128, 128], P(None, 'px', 'py'), may hold values from -6 to 6
- inverse_mass: float32 [384, 128, 128], P('px', 'py'), may hold values from 0.5 to 2
- lame_first: float32 [5, 5, 5, 96, 1024], P(None, None, None, 'px', 'py'), may hold values from 0.5 to 2
- lame_second: float32 [5, 5, 5, 96, 1024], P(None, None, None, 'px', 'py'), may hold values from 0.5 to 2
- level_map: int32 [96, 1024], P('px', 'py'), may hold values from 0 to 2, as said below
Outputs:
- new_displacement: float32 [3, 384, 128, 128], P(None, 'px', 'py')
- new_velocity: float32 [3, 384, 128, 128], P(None, 'px', 'py')
The draws below stay inside these ranges and needn't reach their ends.
Inputs may be any that keep to these rules, and one draw needn't show every extreme that they name: `level_map`: level 2 is the finest. The device whose blocks hold the most finest-level elements holds exactly 96 of them; no device holds more.
All inputs are finite; a program needn't handle non-finite values.
Results may differ from the reference program's by a relative error of at most 0.0003.
Values sent between devices are 32-bit elements; how exact they have to be, the bound alone decides.
A program may use at most 32 MiB of HBM per device.

```python
import math
import jax
import jax.numpy as jnp
import numpy as np
from jax import lax

EX = 1
EY = 4
EZ = 32
LEVELS = 3
SUBSTEPS = 4
EXT = 96
EYT = 32
NXT = 384
NYT = 128
NZ = 128


def draw_level_map(key, part):
    fine_depth = 3 * EZ // 4
    depth_step = max(EZ // 8, 1)
    band_depth = EZ // 4
    rows_devices = EXT // EX
    cols_devices = EYT // EY
    centre_x_key, centre_y_key, rough_key = jax.random.split(key, 3)
    centre_x = jax.random.randint(centre_x_key, (), 0, rows_devices)
    centre_y = jax.random.randint(centre_y_key, (), 0, cols_devices)
    device_x = jnp.arange(EXT, dtype=jnp.int32) // EX
    device_y = jnp.arange(EYT, dtype=jnp.int32) // EY
    distance = jnp.abs(device_x - centre_x)[:, None] + jnp.abs(device_y - centre_y)[None, :]
    distance = jnp.minimum(distance, 4)
    roughness = jax.random.randint(rough_key, (EXT, EYT), 0, depth_step)
    depth = jnp.where(distance == 0, fine_depth, fine_depth - depth_step * distance - roughness)
    layer = jnp.arange(EZ, dtype=jnp.int32)[None, None, :]
    levels = jnp.where(layer < depth[:, :, None], LEVELS - 1, jnp.where(layer < depth[:, :, None] + band_depth, LEVELS - 2, 0))
    return levels.astype(jnp.int32).reshape(EXT, EYT * EZ)


def block_levels(key, dims, cuts, least, largest):
    def one(position, blocks):
        steps = jax.random.uniform(jax.random.fold_in(jax.random.fold_in(key, 6), position), (blocks,), jnp.float32, least / len(cuts), largest / len(cuts))
        return jnp.repeat(jnp.exp(steps), dims[position] // blocks).reshape((-1,) + (1,) * (len(dims) - position - 1))

    factor_of = one(*cuts[0])
    for cut in cuts[1:]:
        factor_of = factor_of * one(*cut)
    return factor_of


def gaussian(key, shape, scale, reach, cuts=(), kind=jnp.bfloat16):
    values = jax.random.normal(key, shape, jnp.float32) * scale
    if len(cuts) > 0:
        values = block_levels(key, shape, cuts, -0.22, 0.18) * values
    return jnp.clip(values, min=-reach, max=reach).astype(kind)


def setup_inputs(seed: int = 0) -> dict:
    key_list = jax.random.split(jax.random.key(seed), 7)
    displacement = gaussian(key_list[0], (3, NXT, NYT, NZ), 1.0, 6.0, ((1, 96), (2, 8)), jnp.float32)
    velocity = gaussian(key_list[1], (3, NXT, NYT, NZ), 1.0, 6.0, ((1, 96), (2, 8)), jnp.float32)
    inverse_mass = jnp.clip(jnp.exp(math.log(2.0) - 1.3862944 * jax.random.uniform(key_list[2], (NXT, NYT, NZ), jnp.float32) ** block_levels(key_list[2], (NXT, NYT, NZ), ((0, 96), (1, 8)), -0.2, 0.2)), 0.5, 2.0)
    lame_first = jnp.clip(jnp.exp(math.log(2.0) - 1.3862944 * jax.random.uniform(key_list[3], (5, 5, 5, EXT, EYT * EZ), jnp.float32) ** block_levels(key_list[3], (5, 5, 5, EXT, EYT * EZ), ((3, 96), (4, 8)), -0.2, 0.2)), 0.5, 2.0)
    lame_second = jnp.clip(jnp.exp(math.log(2.0) - 1.3862944 * jax.random.uniform(key_list[4], (5, 5, 5, EXT, EYT * EZ), jnp.float32) ** block_levels(key_list[4], (5, 5, 5, EXT, EYT * EZ), ((3, 96), (4, 8)), -0.2, 0.2)), 0.5, 2.0)
    level_map = draw_level_map(jax.random.fold_in(key_list[6], 71), 0)
    return {"displacement": displacement, "velocity": velocity, "inverse_mass": inverse_mass, "lame_first": lame_first, "lame_second": lame_second, "level_map": level_map}


time_step = 0.1

def gll_tables():
    points = np.array([-1.0, -np.sqrt(3.0 / 7.0), 0.0, np.sqrt(3.0 / 7.0), 1.0])
    weights = np.array([0.1, 49.0 / 90.0, 32.0 / 45.0, 49.0 / 90.0, 0.1])
    legendre = (35.0 * points ** 4 - 30.0 * points ** 2 + 3.0) / 8.0
    derivative = np.zeros((5, 5))
    for row_index in range(5):
        for col_index in range(5):
            if row_index != col_index:
                derivative[row_index, col_index] = legendre[row_index] / (legendre[col_index] * (points[row_index] - points[col_index]))
    derivative[0, 0] = -5.0
    derivative[4, 4] = 5.0
    return (derivative, weights)

def element_forces(displaced, lame_first, lame_second, derivative, weights):
    matrix_d = jnp.asarray(derivative, jnp.float32)
    gll_weights = jnp.asarray(weights, jnp.float32)
    precise = lax.Precision.HIGHEST
    grad_x = jnp.einsum('ai,cijk...->cajk...', matrix_d, displaced, precision=precise)
    grad_y = jnp.einsum('bj,cijk...->cibk...', matrix_d, displaced, precision=precise)
    grad_z = jnp.einsum('gk,cijk...->cijg...', matrix_d, displaced, precision=precise)
    cube_weights = gll_weights[:, None, None] * gll_weights[None, :, None] * gll_weights[None, None, :]
    cube_weights = cube_weights.reshape((5, 5, 5) + (1,) * (displaced.ndim - 4))
    lame_term = lame_first * cube_weights * (grad_x[0] + grad_y[1] + grad_z[2])
    shear_half = lame_second * cube_weights
    stress_xx = lame_term + 2.0 * shear_half * grad_x[0]
    stress_yy = lame_term + 2.0 * shear_half * grad_y[1]
    stress_zz = lame_term + 2.0 * shear_half * grad_z[2]
    stress_xy = shear_half * (grad_y[0] + grad_x[1])
    stress_xz = shear_half * (grad_z[0] + grad_x[2])
    stress_yz = shear_half * (grad_z[1] + grad_y[2])
    flux_x = jnp.stack([stress_xx, stress_xy, stress_xz])
    flux_y = jnp.stack([stress_xy, stress_yy, stress_yz])
    flux_z = jnp.stack([stress_xz, stress_yz, stress_zz])
    force_x = jnp.einsum('ai,cajk...->cijk...', matrix_d, flux_x, precision=precise)
    force_y = jnp.einsum('bj,cibk...->cijk...', matrix_d, flux_y, precision=precise)
    force_z = jnp.einsum('gk,cijg...->cijk...', matrix_d, flux_z, precision=precise)
    return force_x + force_y + force_z

def expand_axis(nodal_array, dim_index):
    outer_shape = nodal_array.shape[:dim_index]
    inner_shape = nodal_array.shape[dim_index + 1:]
    element_count = (nodal_array.shape[dim_index] - 1) // 4
    leading = lax.slice_in_dim(nodal_array, 0, 4 * element_count, axis=dim_index)
    leading = leading.reshape(outer_shape + (element_count, 4) + inner_shape)
    leading = jnp.moveaxis(leading, dim_index + 1, dim_index)
    trailing = lax.slice_in_dim(nodal_array, 4, 4 * element_count + 1, stride=4, axis=dim_index)
    trailing = jnp.expand_dims(trailing, dim_index)
    return jnp.concatenate([leading, trailing], axis=dim_index)

def collapse_axis(elemental, dim_index):
    outer_shape = elemental.shape[:dim_index]
    inner_shape = elemental.shape[dim_index + 2:]
    element_count = elemental.shape[dim_index + 1]
    leading = lax.slice_in_dim(elemental, 0, 4, axis=dim_index)
    leading = jnp.moveaxis(leading, dim_index, dim_index + 1).reshape(outer_shape + (4 * element_count,) + inner_shape)
    trailing = lax.slice_in_dim(elemental, 4, 5, axis=dim_index)
    zero_block = jnp.zeros_like(lax.slice_in_dim(elemental, 0, 3, axis=dim_index))
    trailing = jnp.concatenate([zero_block, trailing], axis=dim_index)
    trailing = jnp.moveaxis(trailing, dim_index, dim_index + 1).reshape(outer_shape + (4 * element_count,) + inner_shape)
    lead_pad = [(0, 0)] * len(outer_shape) + [(0, 1)] + [(0, 0)] * len(inner_shape)
    trail_pad = [(0, 0)] * len(outer_shape) + [(1, 0)] + [(0, 0)] * len(inner_shape)
    return jnp.pad(leading, lead_pad) + jnp.pad(trailing, trail_pad)

def assembled_force(displacement, lame_first, lame_second, level_map, level_index, derivative, weights):
    padded = jnp.pad(displacement, ((0, 0), (0, 1), (0, 1), (0, 1)))
    column_total = lame_first.shape[3]
    depth_total = displacement.shape[3] // 4
    across_total = lame_first.shape[4] // depth_total

    def slab_force(column):
        start = (column * 4).astype(jnp.int32)
        slab = lax.dynamic_slice_in_dim(padded, start, 5, axis=1)
        spread = expand_axis(expand_axis(slab, 2), 4)
        spread = jnp.transpose(spread, (0, 1, 2, 4, 3, 5)).reshape((3, 5, 5, 5, across_total * depth_total))
        first_slab = lax.dynamic_index_in_dim(lame_first, column, axis=3, keepdims=False)
        second_slab = lax.dynamic_index_in_dim(lame_second, column, axis=3, keepdims=False)
        level_slab = lax.dynamic_index_in_dim(level_map, column, axis=0, keepdims=False)
        chosen = (level_slab == level_index).astype(jnp.float32)
        forces = element_forces(spread, first_slab, second_slab, derivative, weights) * chosen
        forces = forces.reshape((3, 5, 5, 5, across_total, depth_total))
        forces = jnp.transpose(forces, (0, 1, 2, 4, 3, 5))
        nodal_force = collapse_axis(collapse_axis(forces, 4), 2)
        return (nodal_force[:, :4], nodal_force[:, 4])
    leading_parts, trailing_parts = lax.map(slab_force, jnp.arange(column_total, dtype=jnp.int32))
    trailing_shift = jnp.concatenate([jnp.zeros_like(trailing_parts[:1]), trailing_parts[:-1]], axis=0)
    leading_parts = leading_parts.at[:, :, 0].add(trailing_shift)
    nodal_force = jnp.moveaxis(leading_parts, 0, 1).reshape((3, 4 * column_total) + leading_parts.shape[3:])
    return nodal_force[:, :, :displacement.shape[2], :displacement.shape[3]]

def reference(displacement, velocity, inverse_mass, lame_first, lame_second, level_map):
    derivative, weights = gll_tables()
    stored = [None] * LEVELS
    for substep in range(SUBSTEPS):
        for level_index in range(LEVELS):
            if substep % 2 ** (LEVELS - 1 - level_index) == 0:
                stored[level_index] = assembled_force(displacement, lame_first, lame_second, level_map, level_index, derivative, weights)
        total_force = stored[0]
        for level_index in range(1, LEVELS):
            total_force = total_force + stored[level_index]
        velocity = velocity - time_step * inverse_mass[None] * total_force
        displacement = displacement + time_step * velocity
    return (displacement, velocity)
```

```python
import functools

import jax
import jax.numpy as jnp
import ml_dtypes
import numpy as np
from jax import lax
from jax.experimental import pallas as pl
from jax.experimental.pallas import tpu as pltpu
from jax.sharding import PartitionSpec as P

SUBSTEPS = 4
TIME_STEP = 0.1
MESH = pl.DeviceIdType.MESH
F32 = jnp.float32
BF16 = jnp.bfloat16
NEIGHBOURS = [(1, 0), (-1, 0), (1, 1), (1, -1), (-1, 1), (-1, -1), (0, 1), (0, -1)]
SLOT = {d: n for n, d in enumerate(NEIGHBOURS)}
XF, XB, DPP, DPM, DMP, DMM, YU, YD = range(8)


def gll_tables():
    points = np.array([-1.0, -np.sqrt(3.0 / 7.0), 0.0, np.sqrt(3.0 / 7.0), 1.0])
    weights = np.array([0.1, 49.0 / 90.0, 32.0 / 45.0, 49.0 / 90.0, 0.1])
    legendre = (35.0 * points**4 - 30.0 * points**2 + 3.0) / 8.0
    derivative = np.zeros((5, 5))
    for row in range(5):
        for col in range(5):
            if row != col:
                derivative[row, col] = legendre[row] / (legendre[col] * (points[row] - points[col]))
    derivative[0, 0] = -5.0
    derivative[4, 4] = 5.0
    return derivative, weights


def place(k, j):
    if k < 4 and j < 4:
        return k * 4 + j
    return 16 + k if k < 4 else 20 + j


def split_table(table):
    high = table.astype(ml_dtypes.bfloat16)
    low = (table - high.astype(np.float64)).astype(ml_dtypes.bfloat16)
    return high, low


@functools.cache
def tables():
    derivative, weights = gll_tables()
    grads = np.zeros((384, 208))
    cube = np.zeros(384)
    for i in range(5):
        for j in range(5):
            for k in range(5):
                row = i * 25 + j * 5 + k
                for d in range(3):
                    cube[d * 128 + row] = weights[i] * weights[j] * weights[k]
                for n in range(5):
                    grads[row, place(k, j) * 8 + n] += derivative[i, n]
                    grads[128 + row, place(k, n) * 8 + i] += derivative[j, n]
                    grads[256 + row, place(n, j) * 8 + i] += derivative[k, n]
    high, low = split_table(grads)
    first = np.concatenate([high, high, low], axis=1)
    high, low = split_table((grads[:, :200] * cube[:, None]).T)
    second = np.concatenate([high, high, low], axis=1)
    spread = np.zeros((512, 512), ml_dtypes.bfloat16)
    pack = np.zeros((128, 128), ml_dtypes.bfloat16)
    for k in range(4):
        for c in range(32):
            pack[4 * c + k, k * 32 + c] = 1
            for b in range(4):
                spread[b * 128 + 4 * c + k, k * 128 + b * 32 + c] = 1
    return first, second, spread, np.ascontiguousarray(spread.T), pack


def halves(value):
    high = value.astype(BF16)
    return high, (value - high.astype(F32)).astype(BF16)


def permute(value, matrix):
    high, low = halves(value)
    rows = value.shape[0]
    out = jnp.dot(jnp.concatenate([high, low], axis=0), matrix, preferred_element_type=F32)
    return out[:rows] + out[rows:]


def kernel(
    nx,
    ny,
    u_hbm,
    v_hbm,
    im_hbm,
    la_hbm,
    mu_hbm,
    level_hbm,
    first_hbm,
    second_hbm,
    spread_hbm,
    gather_hbm,
    pack_hbm,
    uo_hbm,
    vo_hbm,
    u_vm,
    vim_vm,
    la_vm,
    mu_vm,
    level_vm,
    first_vm,
    second_vm,
    spread_vm,
    gather_vm,
    pack_vm,
    halo_u,
    halo_vim,
    halo_y_send,
    halo_y,
    halo_c_send,
    halo_c,
    x_own,
    x_line,
    u_all,
    v_own,
    im_own,
    u_line,
    v_line,
    im_line,
    u_split,
    s_split,
    f_kept,
    f_sum,
    pack_up,
    pack_down,
    send_x,
    send_d,
    send_y,
    recv_x,
    recv_d,
    recv_y,
    uo_vm,
    vo_vm,
    load_sem,
    halo_send_sem,
    halo_recv_sem,
    send_sem,
    recv_sem,
):
    px, py = lax.axis_index("px"), lax.axis_index("py")

    def present(dx, dy):
        conditions = []
        if dx:
            conditions.append(px < nx - 1 if dx > 0 else px > 0)
        if dy:
            conditions.append(py < ny - 1 if dy > 0 else py > 0)
        return functools.reduce(jnp.logical_and, conditions)

    barrier = pltpu.get_barrier_semaphore()
    for dx, dy in NEIGHBOURS:

        @pl.when(present(dx, dy))
        def _():
            pl.semaphore_signal(barrier, inc=1, device_id=(px + dx, py + dy), device_id_type=MESH)

    loads = []
    for n, (source, target) in enumerate(
        [
            (u_hbm, u_vm),
            (v_hbm, vim_vm.at[0:3]),
            (im_hbm, vim_vm.at[3:4]),
            (spread_hbm, spread_vm),
            (pack_hbm, pack_vm),
            (first_hbm, first_vm),
            (la_hbm, la_vm.at[0:125]),
            (mu_hbm, mu_vm.at[0:125]),
            (second_hbm, second_vm),
            (level_hbm, level_vm),
            (gather_hbm, gather_vm),
        ]
    ):
        loads.append(pltpu.make_async_copy(source, target, load_sem.at[n]))
        loads[-1].start()

    x_own[...] = jnp.zeros_like(x_own)
    x_line[...] = jnp.zeros_like(x_line)
    u_all[...] = jnp.zeros_like(u_all)

    for n, (dx, dy) in enumerate(NEIGHBOURS):

        @pl.when(jnp.logical_not(present(-dx, -dy)))
        def _():
            for s in range(SUBSTEPS):
                if n < 2:
                    recv_x[s, n] = jnp.zeros_like(recv_x[s, n])
                elif n < 6:
                    recv_d[s, n - 2] = jnp.zeros_like(recv_d[s, n - 2])
                else:
                    recv_y[s, n - 6] = jnp.zeros_like(recv_y[s, n - 6])
            if n == XB:
                halo_u[...] = jnp.zeros_like(halo_u)
                halo_vim[...] = jnp.zeros_like(halo_vim)
            if n == YD:
                halo_y[...] = jnp.zeros_like(halo_y)
            if n == DMM:
                halo_c[...] = jnp.zeros_like(halo_c)

    for n in range(3):
        loads[n].wait()
    for c in range(7):
        source = u_vm.at[c] if c < 3 else vim_vm.at[c - 3]
        halo_y_send[4 * c : 4 * c + 4, :] = source[pl.ds(0, 4, stride=16), :]
        halo_c_send[c : c + 1, :] = source[0:1, :]

    def remote(source, target, sems, n, dx, dy):
        send, recv = sems
        return pltpu.make_async_remote_copy(
            src_ref=source,
            dst_ref=target,
            send_sem=send.at[n],
            recv_sem=recv.at[n],
            device_id=(px + dx, py + dy),
            device_id_type=MESH,
        )

    halo_sems = (halo_send_sem, halo_recv_sem)
    halos = [
        remote(u_hbm.at[:, 0:16, :], halo_u, halo_sems, 0, -1, 0),
        remote(halo_c_send, halo_c, halo_sems, 1, -1, -1),
        remote(halo_y_send, halo_y, halo_sems, 2, 0, -1),
        remote(v_hbm.at[:, 0:16, :], halo_vim.at[0:3], halo_sems, 3, -1, 0),
        remote(im_hbm.at[:, 0:16, :], halo_vim.at[3:4], halo_sems, 4, -1, 0),
    ]
    halo_to = [(-1, 0), (-1, -1), (0, -1), (-1, 0), (-1, 0)]

    neighbours = 0
    for dx, dy in NEIGHBOURS:
        neighbours = neighbours + present(dx, dy).astype(jnp.int32)
    pl.semaphore_wait(barrier, neighbours)
    for copy, to in zip(halos, halo_to):

        @pl.when(present(*to))
        def _():
            copy.start()

    def wait_halo(n):
        dx, dy = halo_to[n]

        @pl.when(present(-dx, -dy))
        def _():
            halos[n].wait_recv()

    lane = lax.broadcasted_iota(jnp.int32, (8, 128), 1)
    sublane = lax.broadcasted_iota(jnp.int32, (8, 128), 0)
    depth = lane & 31
    column = lane >> 5

    def fill_own(c, source):
        for j in range(4):
            for b in range(4):
                row = (c * 4 + j) * 8
                x_own[b, row : row + 4, :] = source[pl.ds(4 * b + j, 4, stride=16), :]

    def fill_far(c, source):
        for b in range(4):
            x_own[b, pl.ds(c * 32 + 4, 4, stride=8), :] = source[4 * b : 4 * b + 4, :]

    def spread(first_row, rows):
        wide = jnp.concatenate([x_own[b, first_row : first_row + rows, :] for b in range(4)], axis=1)
        return permute(wide, spread_vm[...])

    for c in range(3):
        fill_own(c, u_vm.at[c])
    for c in range(4):
        fill_own(3 + c, vim_vm.at[c])
    loads[3].wait()
    loads[4].wait()
    for n in range(5, 11):
        loads[n].wait()
    la_vm[125:128, :] = jnp.zeros((3, 128), F32)
    mu_vm[125:128, :] = jnp.zeros((3, 128), F32)

    wait_halo(0)
    wait_halo(1)
    wait_halo(2)
    for c in range(3):
        fill_far(c, halo_u.at[c])
    for c in range(7):
        x_line[c * 8 : c * 8 + 4, :] = halo_y[4 * c : 4 * c + 4, :]
        x_line[c * 8 + 4 : c * 8 + 5, :] = halo_c[c : c + 1, :]
    nodes = spread(0, 96)
    for c in range(3):
        for j in range(4):
            for k in range(4):
                row = (c * 4 + j) * 8
                u_all[c, (k * 4 + j) * 8 : (k * 4 + j + 1) * 8, :] = nodes[row : row + 8, k * 128 : (k + 1) * 128]
    lines = permute(x_line[...], pack_vm[...])
    u_line[...] = lines[0:24]
    v_line[...] = lines[24:48]
    im_line[...] = TIME_STEP * lines[48:56]

    def group(p):
        return pl.ds(p * 8, 8)

    def expand():
        for c in range(3):
            line = u_line[c * 8 : c * 8 + 8, :]
            for k in range(4):
                inner = pltpu.roll(u_all[c, group(k * 4), :], 96, 1)
                outer = pltpu.roll(line, (96 - 32 * k) % 128, 1) if k != 3 else line
                u_all[c, group(16 + k), :] = jnp.where(column == 3, outer, inner)
            for j in range(5):
                below = pltpu.roll(u_all[c, group(j if j < 4 else 16), :], 127, 1)
                u_all[c, group(20 + j), :] = jnp.where(depth < 31, below, 0.0)

    def forces(s):
        for c in range(3):
            high, low = halves(u_all[c])
            lanes = slice(c * 128, (c + 1) * 128)
            u_split[0:208, lanes] = high
            u_split[208:416, lanes] = low
            u_split[416:624, lanes] = high
        grads = jnp.dot(first_vm[...], u_split[...], preferred_element_type=F32)

        def grad(c, d):
            return grads[d * 128 : (d + 1) * 128, c * 128 : (c + 1) * 128]

        first, second = la_vm[...], mu_vm[...]
        pressure = first * (grad(0, 0) + grad(1, 1) + grad(2, 2))
        for c in range(3):
            for d in range(c, 3):
                if c == d:
                    stress = pressure + 2.0 * second * grad(c, c)
                else:
                    stress = second * (grad(c, d) + grad(d, c))
                high, low = halves(stress)
                for e, f in ((c, d), (d, c))[: 1 + (c != d)]:
                    lanes = slice(e * 128, (e + 1) * 128)
                    s_split[f * 128 : (f + 1) * 128, lanes] = high
                    s_split[384 + f * 128 : 384 + (f + 1) * 128, lanes] = low
                    s_split[768 + f * 128 : 768 + (f + 1) * 128, lanes] = high
        out = jnp.dot(second_vm[...], s_split[...], preferred_element_type=F32)
        least = jnp.where(s == 0, 0, jnp.where(s == 2, 1, 2))
        active = level_vm[...] >= least
        for c in range(3):
            new = out[:, c * 128 : (c + 1) * 128]
            f_kept[c] = jnp.where(active, new, f_kept[c])

    def assemble(s, last):
        for c in range(3):
            f = [f_kept[c, group(p), :] for p in range(25)]
            for j in range(5):
                p = j if j < 4 else 16
                f[p] = f[p] + jnp.where(depth > 0, pltpu.roll(f[20 + j], 1, 1), 0.0)
            up = jnp.zeros((8, 128), F32)
            down = jnp.zeros((8, 128), F32)
            for k in range(4):
                shifted = pltpu.roll(f[16 + k], 32, 1)
                up = jnp.where(column == k, pltpu.roll(shifted, 32 * k, 1) if k else shifted, up)
                down = jnp.where(column == k, pltpu.roll(f[4 * k], 32 * k, 1) if k else f[0], down)
                f[4 * k] = f[4 * k] + jnp.where(column > 0, shifted, 0.0)
            for p in range(16):
                f_sum[c, group(p), :] = f[p]
            pack_up[c * 8 : c * 8 + 8, :] = up
            pack_down[c * 8 : c * 8 + 8, :] = down
        for c in range(3):
            send_x[s, XF, c * 16 : c * 16 + 16, :] = f_sum[c, pl.ds(4, 16, stride=8), :]
            if not last:
                send_x[s, XB, c * 16 : c * 16 + 16, :] = f_sum[c, pl.ds(0, 16, stride=8), :]
        up_far = pack_up[pl.ds(4, 3, stride=8), :]
        send_d[s, DPP - 2, 0:3, :] = up_far
        send_y[s, 0] = pack_up[...]
        if not last:
            up_near = pack_up[pl.ds(0, 3, stride=8), :]
            send_d[s, DPM - 2, 0:3, :] = pack_down[pl.ds(4, 3, stride=8), :]
            send_d[s, DMP - 2, 0:3, :] = up_near
            send_d[s, DMM - 2, 0:3, :] = pack_down[pl.ds(0, 3, stride=8), :]
            send_x[s, XF, 48:51, :] = up_far
            send_x[s, XB, 48:51, :] = up_near
            send_y[s, 1] = pack_down[...]

    def exchange(s, last):
        copies = []
        for n, (dx, dy) in enumerate(NEIGHBOURS):
            if last and (dx < 0 or dy < 0):
                continue
            if n < 2:
                pair = (send_x.at[s, n], recv_x.at[s, n])
            elif n < 6:
                pair = (send_d.at[s, n - 2], recv_d.at[s, n - 2])
            else:
                pair = (send_y.at[s, n - 6], recv_y.at[s, n - 6])
            copies.append(((dx, dy), remote(*pair, (send_sem.at[s], recv_sem.at[s]), n, dx, dy)))
        return copies

    def start(copies):
        for to, copy in copies:

            @pl.when(present(*to))
            def _():
                copy.start()

    def arrive(copies):
        for (dx, dy), copy in copies:

            @pl.when(present(-dx, -dy))
            def _():
                copy.wait_recv()

    def finish(copies):
        for to, copy in copies:

            @pl.when(present(*to))
            def _():
                copy.wait_send()

    def advance(s, last):
        for c in range(3):
            near = recv_y[s, 0, c * 8 : c * 8 + 8, :]
            near = near + jnp.where(sublane == 0, recv_d[s, DPP - 2, c : c + 1, :], 0.0)
            if not last:
                near = near + jnp.where(sublane == 4, recv_d[s, DMP - 2, c : c + 1, :], 0.0)
            for k in range(4):
                part = pltpu.roll(near, 128 - 32 * k, 1) if k else near
                f_sum[c, group(4 * k), :] = f_sum[c, group(4 * k), :] + jnp.where(column == 0, part, 0.0)
            f_sum[c, pl.ds(0, 16, stride=8), :] = f_sum[c, pl.ds(0, 16, stride=8), :] + recv_x[s, XF, c * 16 : c * 16 + 16, :]
            if not last:
                f_sum[c, pl.ds(4, 16, stride=8), :] = (
                    f_sum[c, pl.ds(4, 16, stride=8), :] + recv_x[s, XB, c * 16 : c * 16 + 16, :]
                )
        for c in range(3):
            v = v_own[c] - im_own[...] * f_sum[c]
            v_own[c] = v
            u_all[c, 0:128, :] = u_all[c, 0:128, :] + TIME_STEP * v
        if last:
            return
        for c in range(3):
            rows = slice(c * 8, c * 8 + 8)
            far = pack_up[rows, :] + recv_y[s, 1, rows, :]
            left = recv_x[s, XF, 48 + c : 49 + c, :] + recv_d[s, DPM - 2, c : c + 1, :]
            right = recv_x[s, XB, 48 + c : 49 + c, :] + recv_d[s, DMM - 2, c : c + 1, :]
            far = far + jnp.where(sublane == 0, left, 0.0) + jnp.where(sublane == 4, right, 0.0)
            v = v_line[rows, :] - im_line[...] * far
            v_line[rows, :] = v
            u_line[rows, :] = u_line[rows, :] + TIME_STEP * v
        expand()

    def late_nodes():
        wait_halo(3)
        wait_halo(4)
        for c in range(4):
            fill_far(3 + c, halo_vim.at[c])
        values = spread(96, 128)
        for c in range(4):
            for j in range(4):
                for k in range(4):
                    row = (c * 4 + j) * 8
                    value = values[row : row + 8, k * 128 : (k + 1) * 128]
                    if c < 3:
                        v_own[c, group(k * 4 + j), :] = value
                    else:
                        im_own[group(k * 4 + j), :] = TIME_STEP * value

    expand()
    forces(0)
    assemble(0, False)
    copies = exchange(0, False)
    start(copies)
    late_nodes()
    arrive(copies)
    advance(0, False)

    def substep(s, carry):
        forces(s)
        assemble(s, False)
        copies = exchange(s, False)
        start(copies)
        arrive(copies)
        advance(s, False)
        return carry

    lax.fori_loop(1, SUBSTEPS - 1, substep, 0)
    s = SUBSTEPS - 1
    forces(s)
    assemble(s, True)
    copies = exchange(s, True)
    start(copies)
    arrive(copies)
    advance(s, True)

    rows = []
    for source in (u_all, v_own):
        for c in range(3):
            for j in range(4):
                rows.append(jnp.concatenate([source[c, group(k * 4 + j), :] for k in range(4)], axis=1))
    result = permute(jnp.concatenate(rows, axis=0), gather_vm[...])
    for a, target in enumerate((uo_vm, vo_vm)):
        for c in range(3):
            for j in range(4):
                row = ((a * 3 + c) * 4 + j) * 8
                for b in range(4):
                    target[c, pl.ds(4 * b + j, 4, stride=16), :] = result[row : row + 4, b * 128 : (b + 1) * 128]
    stores = [
        pltpu.make_async_copy(uo_vm, uo_hbm, load_sem.at[0]),
        pltpu.make_async_copy(vo_vm, vo_hbm, load_sem.at[1]),
    ]
    for copy in stores:
        copy.start()
    for copy, to in zip(halos, halo_to):

        @pl.when(present(*to))
        def _():
            copy.wait_send()

    def drain(s, carry):
        finish(exchange(s, False))
        return carry

    lax.fori_loop(0, SUBSTEPS - 1, drain, 0)
    finish(exchange(SUBSTEPS - 1, True))
    for copy in stores:
        copy.wait()


def shards(nx, ny, displacement, velocity, inverse_mass, lame_first, lame_second, level_map):
    first, second, spread, gather, pack = (jnp.asarray(table) for table in tables())
    vmem = pltpu.VMEM
    uo, vo = pl.pallas_call(
        functools.partial(kernel, nx, ny),
        out_shape=[jax.ShapeDtypeStruct((3, 64, 128), F32)] * 2,
        in_specs=[pl.BlockSpec(memory_space=pl.ANY)] * 11,
        out_specs=[pl.BlockSpec(memory_space=pl.ANY)] * 2,
        scratch_shapes=[
            vmem((3, 64, 128), F32),
            vmem((4, 64, 128), F32),
            vmem((128, 128), F32),
            vmem((128, 128), F32),
            vmem((1, 128), jnp.int32),
            vmem((384, 624), BF16),
            vmem((200, 1152), BF16),
            vmem((512, 512), BF16),
            vmem((512, 512), BF16),
            vmem((128, 128), BF16),
            vmem((3, 16, 128), F32),
            vmem((4, 16, 128), F32),
            vmem((32, 128), F32),
            vmem((32, 128), F32),
            vmem((8, 128), F32),
            vmem((8, 128), F32),
            vmem((4, 224, 128), F32),
            vmem((56, 128), F32),
            vmem((3, 208, 128), F32),
            vmem((3, 128, 128), F32),
            vmem((128, 128), F32),
            vmem((24, 128), F32),
            vmem((24, 128), F32),
            vmem((8, 128), F32),
            vmem((624, 384), BF16),
            vmem((1152, 384), BF16),
            vmem((3, 200, 128), F32),
            vmem((3, 128, 128), F32),
            vmem((24, 128), F32),
            vmem((24, 128), F32),
            vmem((SUBSTEPS, 2, 56, 128), F32),
            vmem((SUBSTEPS, 4, 8, 128), F32),
            vmem((SUBSTEPS, 2, 24, 128), F32),
            vmem((SUBSTEPS, 2, 56, 128), F32),
            vmem((SUBSTEPS, 4, 8, 128), F32),
            vmem((SUBSTEPS, 2, 24, 128), F32),
            vmem((3, 64, 128), F32),
            vmem((3, 64, 128), F32),
            pltpu.SemaphoreType.DMA((11,)),
            pltpu.SemaphoreType.DMA((5,)),
            pltpu.SemaphoreType.DMA((5,)),
            pltpu.SemaphoreType.DMA((SUBSTEPS, 8)),
            pltpu.SemaphoreType.DMA((SUBSTEPS, 8)),
        ],
        compiler_params=pltpu.CompilerParams(collective_id=0, has_side_effects=True),
        name="substeps",
    )(
        displacement.reshape(3, 64, 128),
        velocity.reshape(3, 64, 128),
        inverse_mass.reshape(1, 64, 128),
        lame_first.reshape(125, 128),
        lame_second.reshape(125, 128),
        level_map,
        first,
        second,
        spread,
        gather,
        pack,
    )
    return uo.reshape(3, 4, 16, 128), vo.reshape(3, 4, 16, 128)


def solution(mesh):
    in_specs = (
        P(None, "px", "py", None),
        P(None, "px", "py", None),
        P("px", "py", None),
        P(None, None, None, "px", "py"),
        P(None, None, None, "px", "py"),
        P("px", "py"),
    )
    out_specs = (P(None, "px", "py", None), P(None, "px", "py", None))
    body = functools.partial(shards, mesh.shape["px"], mesh.shape["py"])
    return jax.shard_map(body, mesh=mesh, in_specs=in_specs, out_specs=out_specs, check_vma=False)
```

```python
import functools

import jax
import jax.numpy as jnp
import ml_dtypes
import numpy as np
from jax import lax
from jax.experimental import pallas as pl
from jax.experimental.pallas import tpu as pltpu
from jax.sharding import PartitionSpec as P

SUBSTEPS = 4
TIME_STEP = 0.1
MESH = pl.DeviceIdType.MESH
F32 = jnp.float32
BF16 = jnp.bfloat16
NEIGHBOURS = [(1, 0), (-1, 0), (1, 1), (1, -1), (-1, 1), (-1, -1), (0, 1), (0, -1)]
SLOT = {d: n for n, d in enumerate(NEIGHBOURS)}
XF, XB, DPP, DPM, DMP, DMM, YU, YD = range(8)


def gll_tables():
    points = np.array([-1.0, -np.sqrt(3.0 / 7.0), 0.0, np.sqrt(3.0 / 7.0), 1.0])
    weights = np.array([0.1, 49.0 / 90.0, 32.0 / 45.0, 49.0 / 90.0, 0.1])
    legendre = (35.0 * points**4 - 30.0 * points**2 + 3.0) / 8.0
    derivative = np.zeros((5, 5))
    for row in range(5):
        for col in range(5):
            if row != col:
                derivative[row, col] = legendre[row] / (legendre[col] * (points[row] - points[col]))
    derivative[0, 0] = -5.0
    derivative[4, 4] = 5.0
    return derivative, weights


def place(k, j):
    if k < 4 and j < 4:
        return k * 4 + j
    return 16 + k if k < 4 else 20 + j


@functools.cache
def tables():
    spread = np.zeros((512, 512), ml_dtypes.bfloat16)
    pack = np.zeros((128, 128), ml_dtypes.bfloat16)
    for k in range(4):
        for c in range(32):
            pack[4 * c + k, k * 32 + c] = 1
            for b in range(4):
                spread[b * 128 + 4 * c + k, k * 128 + b * 32 + c] = 1
    return spread, np.ascontiguousarray(spread.T), pack


def apply(matrix, v):
    even0, odd0 = v[0] + v[4], v[0] - v[4]
    even1, odd1 = v[1] + v[3], v[1] - v[3]
    out = [None] * 5
    for a in range(2):
        row = matrix[a]
        first = float(row[0] - row[4]) / 2 * odd0 + float(row[1] - row[3]) / 2 * odd1
        second = float(row[0] + row[4]) / 2 * even0 + float(row[1] + row[3]) / 2 * even1 + float(row[2]) * v[2]
        out[a], out[4 - a] = first + second, first - second
    out[2] = float(matrix[2][0]) * odd0 + float(matrix[2][1]) * odd1
    return out


def halves(value):
    high = value.astype(BF16)
    return high, (value - high.astype(F32)).astype(BF16)


def permute(value, matrix):
    high, low = halves(value)
    rows = value.shape[0]
    out = jnp.dot(jnp.concatenate([high, low], axis=0), matrix, preferred_element_type=F32)
    return out[:rows] + out[rows:]


def kernel(
    nx,
    ny,
    u_hbm,
    v_hbm,
    im_hbm,
    la_hbm,
    mu_hbm,
    level_hbm,
    spread_hbm,
    gather_hbm,
    pack_hbm,
    uo_hbm,
    vo_hbm,
    u_vm,
    vim_vm,
    la_raw,
    mu_raw,
    la_vm,
    mu_vm,
    mu_twice,
    level_vm,
    spread_vm,
    gather_vm,
    pack_vm,
    halo_u,
    halo_vim,
    halo_y_send,
    halo_y,
    halo_c_send,
    halo_c,
    x_own,
    x_line,
    u_all,
    v_own,
    im_own,
    u_line,
    v_line,
    im_line,
    grad_z,
    stress_x,
    f_new,
    f_kept,
    f_sum,
    pack_up,
    pack_down,
    send_x,
    send_d,
    send_y,
    recv_x,
    recv_d,
    recv_y,
    uo_vm,
    vo_vm,
    load_sem,
    halo_send_sem,
    halo_recv_sem,
    send_sem,
    recv_sem,
):
    px, py = lax.axis_index("px"), lax.axis_index("py")

    def present(dx, dy):
        conditions = []
        if dx:
            conditions.append(px < nx - 1 if dx > 0 else px > 0)
        if dy:
            conditions.append(py < ny - 1 if dy > 0 else py > 0)
        return functools.reduce(jnp.logical_and, conditions)

    barrier = pltpu.get_barrier_semaphore()
    for dx, dy in NEIGHBOURS:

        @pl.when(present(dx, dy))
        def _():
            pl.semaphore_signal(barrier, inc=1, device_id=(px + dx, py + dy), device_id_type=MESH)

    loads = []
    for n, (source, target) in enumerate(
        [
            (u_hbm, u_vm),
            (v_hbm, vim_vm.at[0:3]),
            (im_hbm, vim_vm.at[3:4]),
            (spread_hbm, spread_vm),
            (pack_hbm, pack_vm),
            (la_hbm, la_raw),
            (mu_hbm, mu_raw),
            (level_hbm, level_vm),
            (gather_hbm, gather_vm),
        ]
    ):
        loads.append(pltpu.make_async_copy(source, target, load_sem.at[n]))
        loads[-1].start()

    x_own[...] = jnp.zeros_like(x_own)
    x_line[...] = jnp.zeros_like(x_line)
    u_all[...] = jnp.zeros_like(u_all)

    for n, (dx, dy) in enumerate(NEIGHBOURS):

        @pl.when(jnp.logical_not(present(-dx, -dy)))
        def _():
            for s in range(SUBSTEPS):
                if n < 2:
                    recv_x[s, n] = jnp.zeros_like(recv_x[s, n])
                elif n < 6:
                    recv_d[s, n - 2] = jnp.zeros_like(recv_d[s, n - 2])
                else:
                    recv_y[s, n - 6] = jnp.zeros_like(recv_y[s, n - 6])
            if n == XB:
                halo_u[...] = jnp.zeros_like(halo_u)
                halo_vim[...] = jnp.zeros_like(halo_vim)
            if n == YD:
                halo_y[...] = jnp.zeros_like(halo_y)
            if n == DMM:
                halo_c[...] = jnp.zeros_like(halo_c)

    for n in range(3):
        loads[n].wait()
    for c in range(7):
        source = u_vm.at[c] if c < 3 else vim_vm.at[c - 3]
        halo_y_send[4 * c : 4 * c + 4, :] = source[pl.ds(0, 4, stride=16), :]
        halo_c_send[c : c + 1, :] = source[0:1, :]

    def remote(source, target, sems, n, dx, dy):
        send, recv = sems
        return pltpu.make_async_remote_copy(
            src_ref=source,
            dst_ref=target,
            send_sem=send.at[n],
            recv_sem=recv.at[n],
            device_id=(px + dx, py + dy),
            device_id_type=MESH,
        )

    halo_sems = (halo_send_sem, halo_recv_sem)
    halos = [
        remote(u_hbm.at[:, 0:16, :], halo_u, halo_sems, 0, -1, 0),
        remote(halo_c_send, halo_c, halo_sems, 1, -1, -1),
        remote(halo_y_send, halo_y, halo_sems, 2, 0, -1),
        remote(v_hbm.at[:, 0:16, :], halo_vim.at[0:3], halo_sems, 3, -1, 0),
        remote(im_hbm.at[:, 0:16, :], halo_vim.at[3:4], halo_sems, 4, -1, 0),
    ]
    halo_to = [(-1, 0), (-1, -1), (0, -1), (-1, 0), (-1, 0)]

    neighbours = 0
    for dx, dy in NEIGHBOURS:
        neighbours = neighbours + present(dx, dy).astype(jnp.int32)
    pl.semaphore_wait(barrier, neighbours)
    for copy, to in zip(halos, halo_to):

        @pl.when(present(*to))
        def _():
            copy.start()

    def wait_halo(n):
        dx, dy = halo_to[n]

        @pl.when(present(-dx, -dy))
        def _():
            halos[n].wait_recv()

    lane = lax.broadcasted_iota(jnp.int32, (8, 128), 1)
    sublane = lax.broadcasted_iota(jnp.int32, (8, 128), 0)
    depth = lane & 31
    column = lane >> 5

    def fill_own(c, source):
        for j in range(4):
            for b in range(4):
                row = (c * 4 + j) * 8
                x_own[b, row : row + 4, :] = source[pl.ds(4 * b + j, 4, stride=16), :]

    def fill_far(c, source):
        for b in range(4):
            x_own[b, pl.ds(c * 32 + 4, 4, stride=8), :] = source[4 * b : 4 * b + 4, :]

    def spread(first_row, rows):
        wide = jnp.concatenate([x_own[b, first_row : first_row + rows, :] for b in range(4)], axis=1)
        return permute(wide, spread_vm[...])

    for c in range(3):
        fill_own(c, u_vm.at[c])
    for c in range(4):
        fill_own(3 + c, vim_vm.at[c])
    loads[3].wait()
    loads[4].wait()
    for n in range(5, 9):
        loads[n].wait()
    derivative, weights = gll_tables()
    la_vm[...] = jnp.zeros_like(la_vm)
    mu_vm[...] = jnp.zeros_like(mu_vm)
    for k in range(5):
        for j in range(5):
            for i in range(5):
                weight = float(weights[i] * weights[j] * weights[k])
                row = (k * 5 + j) * 8 + i
                la_vm[row : row + 1, :] = weight * la_raw[i, j, k]
                mu_vm[row : row + 1, :] = weight * mu_raw[i, j, k]
    mu_twice[...] = 2.0 * mu_vm[...]

    wait_halo(0)
    wait_halo(1)
    wait_halo(2)
    for c in range(3):
        fill_far(c, halo_u.at[c])
    for c in range(7):
        x_line[c * 8 : c * 8 + 4, :] = halo_y[4 * c : 4 * c + 4, :]
        x_line[c * 8 + 4 : c * 8 + 5, :] = halo_c[c : c + 1, :]
    nodes = spread(0, 96)
    for c in range(3):
        for j in range(4):
            for k in range(4):
                row = (c * 4 + j) * 8
                u_all[c, (k * 4 + j) * 8 : (k * 4 + j + 1) * 8, :] = nodes[row : row + 8, k * 128 : (k + 1) * 128]
    lines = permute(x_line[...], pack_vm[...])
    u_line[...] = lines[0:24]
    v_line[...] = lines[24:48]
    im_line[...] = TIME_STEP * lines[48:56]

    def group(p):
        return pl.ds(p * 8, 8)

    def expand():
        for c in range(3):
            line = u_line[c * 8 : c * 8 + 8, :]
            for k in range(4):
                inner = pltpu.roll(u_all[c, group(k * 4), :], 96, 1)
                outer = pltpu.roll(line, (96 - 32 * k) % 128, 1) if k != 3 else line
                u_all[c, group(16 + k), :] = jnp.where(column == 3, outer, inner)
            for j in range(5):
                below = pltpu.roll(u_all[c, group(j if j < 4 else 16), :], 127, 1)
                u_all[c, group(20 + j), :] = jnp.where(depth < 31, below, 0.0)

    def columns(matrix):
        out = []
        for n in range(5):
            values = jnp.zeros((8, 128), F32)
            for i in range(5):
                values = jnp.where(sublane == i, float(matrix[i][n]), values)
            out.append(values)
        return out

    def along_x(vectors, ref, c, row):
        total = vectors[0] * jnp.broadcast_to(ref[c, row : row + 1, :], (8, 128))
        for n in range(1, 5):
            total = total + vectors[n] * jnp.broadcast_to(ref[c, row + n : row + n + 1, :], (8, 128))
        return total

    def forces(s):
        forward, backward = columns(derivative), columns(derivative.T)
        for c in range(3):
            for j in range(5):
                out = apply(derivative, [u_all[c, group(place(k, j)), :] for k in range(5)])
                for k in range(5):
                    grad_z[c, group(k * 5 + j), :] = out[k]
        for k in range(5):
            gy = [apply(derivative, [u_all[c, group(place(k, j)), :] for j in range(5)]) for c in range(3)]
            stress_y = [[], [], []]
            for j in range(5):
                rows = group(k * 5 + j)
                gx = [along_x(forward, u_all, c, place(k, j) * 8) for c in range(3)]
                gz = [grad_z[c, rows, :] for c in range(3)]
                first, second, twice = la_vm[rows, :], mu_vm[rows, :], mu_twice[rows, :]
                pressure = first * (gx[0] + gy[1][j] + gz[2])
                xy = second * (gy[0][j] + gx[1])
                xz = second * (gz[0] + gx[2])
                yz = second * (gz[1] + gy[2][j])
                stress_x[0, rows, :] = pressure + twice * gx[0]
                stress_x[1, rows, :] = xy
                stress_x[2, rows, :] = xz
                stress_y[0].append(xy)
                stress_y[1].append(pressure + twice * gy[1][j])
                stress_y[2].append(yz)
                grad_z[0, rows, :] = xz
                grad_z[1, rows, :] = yz
                grad_z[2, rows, :] = pressure + twice * gz[2]
            for c in range(3):
                out = apply(derivative.T, stress_y[c])
                for j in range(5):
                    f_new[c, group(k * 5 + j), :] = out[j] + along_x(backward, stress_x, c, (k * 5 + j) * 8)
        least = jnp.where(s == 0, 0, jnp.where(s == 2, 1, 2))
        active = jnp.broadcast_to(level_vm[...], (8, 128)) >= least
        for c in range(3):
            for j in range(5):
                out = apply(derivative.T, [grad_z[c, group(k * 5 + j), :] for k in range(5)])
                for k in range(5):
                    new = f_new[c, group(k * 5 + j), :] + out[k]
                    rows = group(place(k, j))
                    f_kept[c, rows, :] = jnp.where(active, new, f_kept[c, rows, :])

    def assemble(s, last):
        for c in range(3):
            f = [f_kept[c, group(p), :] for p in range(25)]
            for j in range(5):
                p = j if j < 4 else 16
                f[p] = f[p] + jnp.where(depth > 0, pltpu.roll(f[20 + j], 1, 1), 0.0)
            up = jnp.zeros((8, 128), F32)
            down = jnp.zeros((8, 128), F32)
            for k in range(4):
                shifted = pltpu.roll(f[16 + k], 32, 1)
                up = jnp.where(column == k, pltpu.roll(shifted, 32 * k, 1) if k else shifted, up)
                down = jnp.where(column == k, pltpu.roll(f[4 * k], 32 * k, 1) if k else f[0], down)
                f[4 * k] = f[4 * k] + jnp.where(column > 0, shifted, 0.0)
            for p in range(16):
                f_sum[c, group(p), :] = f[p]
            pack_up[c * 8 : c * 8 + 8, :] = up
            pack_down[c * 8 : c * 8 + 8, :] = down
        for c in range(3):
            send_x[s, XF, c * 16 : c * 16 + 16, :] = f_sum[c, pl.ds(4, 16, stride=8), :]
            if not last:
                send_x[s, XB, c * 16 : c * 16 + 16, :] = f_sum[c, pl.ds(0, 16, stride=8), :]
        up_far = pack_up[pl.ds(4, 3, stride=8), :]
        send_d[s, DPP - 2, 0:3, :] = up_far
        send_y[s, 0] = pack_up[...]
        if not last:
            up_near = pack_up[pl.ds(0, 3, stride=8), :]
            send_d[s, DPM - 2, 0:3, :] = pack_down[pl.ds(4, 3, stride=8), :]
            send_d[s, DMP - 2, 0:3, :] = up_near
            send_d[s, DMM - 2, 0:3, :] = pack_down[pl.ds(0, 3, stride=8), :]
            send_x[s, XF, 48:51, :] = up_far
            send_x[s, XB, 48:51, :] = up_near
            send_y[s, 1] = pack_down[...]

    def exchange(s, last):
        copies = []
        for n, (dx, dy) in enumerate(NEIGHBOURS):
            if last and (dx < 0 or dy < 0):
                continue
            if n < 2:
                pair = (send_x.at[s, n], recv_x.at[s, n])
            elif n < 6:
                pair = (send_d.at[s, n - 2], recv_d.at[s, n - 2])
            else:
                pair = (send_y.at[s, n - 6], recv_y.at[s, n - 6])
            copies.append(((dx, dy), remote(*pair, (send_sem.at[s], recv_sem.at[s]), n, dx, dy)))
        return copies

    def start(copies):
        for to, copy in copies:

            @pl.when(present(*to))
            def _():
                copy.start()

    def arrive(copies):
        for (dx, dy), copy in copies:

            @pl.when(present(-dx, -dy))
            def _():
                copy.wait_recv()

    def finish(copies):
        for to, copy in copies:

            @pl.when(present(*to))
            def _():
                copy.wait_send()

    def advance(s, last):
        for c in range(3):
            near = recv_y[s, 0, c * 8 : c * 8 + 8, :]
            near = near + jnp.where(sublane == 0, recv_d[s, DPP - 2, c : c + 1, :], 0.0)
            if not last:
                near = near + jnp.where(sublane == 4, recv_d[s, DMP - 2, c : c + 1, :], 0.0)
            for k in range(4):
                part = pltpu.roll(near, 128 - 32 * k, 1) if k else near
                f_sum[c, group(4 * k), :] = f_sum[c, group(4 * k), :] + jnp.where(column == 0, part, 0.0)
            f_sum[c, pl.ds(0, 16, stride=8), :] = f_sum[c, pl.ds(0, 16, stride=8), :] + recv_x[s, XF, c * 16 : c * 16 + 16, :]
            if not last:
                f_sum[c, pl.ds(4, 16, stride=8), :] = (
                    f_sum[c, pl.ds(4, 16, stride=8), :] + recv_x[s, XB, c * 16 : c * 16 + 16, :]
                )
        for c in range(3):
            v = v_own[c] - im_own[...] * f_sum[c]
            v_own[c] = v
            u_all[c, 0:128, :] = u_all[c, 0:128, :] + TIME_STEP * v
        if last:
            return
        for c in range(3):
            rows = slice(c * 8, c * 8 + 8)
            far = pack_up[rows, :] + recv_y[s, 1, rows, :]
            left = recv_x[s, XF, 48 + c : 49 + c, :] + recv_d[s, DPM - 2, c : c + 1, :]
            right = recv_x[s, XB, 48 + c : 49 + c, :] + recv_d[s, DMM - 2, c : c + 1, :]
            far = far + jnp.where(sublane == 0, left, 0.0) + jnp.where(sublane == 4, right, 0.0)
            v = v_line[rows, :] - im_line[...] * far
            v_line[rows, :] = v
            u_line[rows, :] = u_line[rows, :] + TIME_STEP * v
        expand()

    def late_nodes():
        wait_halo(3)
        wait_halo(4)
        for c in range(4):
            fill_far(3 + c, halo_vim.at[c])
        values = spread(96, 128)
        for c in range(4):
            for j in range(4):
                for k in range(4):
                    row = (c * 4 + j) * 8
                    value = values[row : row + 8, k * 128 : (k + 1) * 128]
                    if c < 3:
                        v_own[c, group(k * 4 + j), :] = value
                    else:
                        im_own[group(k * 4 + j), :] = TIME_STEP * value

    expand()
    forces(0)
    assemble(0, False)
    copies = exchange(0, False)
    start(copies)
    late_nodes()
    arrive(copies)
    advance(0, False)

    def substep(s, carry):
        forces(s)
        assemble(s, False)
        copies = exchange(s, False)
        start(copies)
        arrive(copies)
        advance(s, False)
        return carry

    lax.fori_loop(1, SUBSTEPS - 1, substep, 0)
    s = SUBSTEPS - 1
    forces(s)
    assemble(s, True)
    copies = exchange(s, True)
    start(copies)
    arrive(copies)
    advance(s, True)

    rows = []
    for source in (u_all, v_own):
        for c in range(3):
            for j in range(4):
                rows.append(jnp.concatenate([source[c, group(k * 4 + j), :] for k in range(4)], axis=1))
    result = permute(jnp.concatenate(rows, axis=0), gather_vm[...])
    for a, target in enumerate((uo_vm, vo_vm)):
        for c in range(3):
            for j in range(4):
                row = ((a * 3 + c) * 4 + j) * 8
                for b in range(4):
                    target[c, pl.ds(4 * b + j, 4, stride=16), :] = result[row : row + 4, b * 128 : (b + 1) * 128]
    stores = [
        pltpu.make_async_copy(uo_vm, uo_hbm, load_sem.at[0]),
        pltpu.make_async_copy(vo_vm, vo_hbm, load_sem.at[1]),
    ]
    for copy in stores:
        copy.start()
    for copy, to in zip(halos, halo_to):

        @pl.when(present(*to))
        def _():
            copy.wait_send()

    def drain(s, carry):
        finish(exchange(s, False))
        return carry

    lax.fori_loop(0, SUBSTEPS - 1, drain, 0)
    finish(exchange(SUBSTEPS - 1, True))
    for copy in stores:
        copy.wait()


def shards(nx, ny, displacement, velocity, inverse_mass, lame_first, lame_second, level_map):
    spread, gather, pack = (jnp.asarray(table) for table in tables())
    vmem = pltpu.VMEM
    uo, vo = pl.pallas_call(
        functools.partial(kernel, nx, ny),
        out_shape=[jax.ShapeDtypeStruct((3, 64, 128), F32)] * 2,
        in_specs=[pl.BlockSpec(memory_space=pl.ANY)] * 9,
        out_specs=[pl.BlockSpec(memory_space=pl.ANY)] * 2,
        scratch_shapes=[
            vmem((3, 64, 128), F32),
            vmem((4, 64, 128), F32),
            vmem((5, 5, 5, 1, 128), F32),
            vmem((5, 5, 5, 1, 128), F32),
            vmem((200, 128), F32),
            vmem((200, 128), F32),
            vmem((200, 128), F32),
            vmem((1, 128), jnp.int32),
            vmem((512, 512), BF16),
            vmem((512, 512), BF16),
            vmem((128, 128), BF16),
            vmem((3, 16, 128), F32),
            vmem((4, 16, 128), F32),
            vmem((32, 128), F32),
            vmem((32, 128), F32),
            vmem((8, 128), F32),
            vmem((8, 128), F32),
            vmem((4, 224, 128), F32),
            vmem((56, 128), F32),
            vmem((3, 200, 128), F32),
            vmem((3, 128, 128), F32),
            vmem((128, 128), F32),
            vmem((24, 128), F32),
            vmem((24, 128), F32),
            vmem((8, 128), F32),
            vmem((3, 200, 128), F32),
            vmem((3, 200, 128), F32),
            vmem((3, 200, 128), F32),
            vmem((3, 200, 128), F32),
            vmem((3, 128, 128), F32),
            vmem((24, 128), F32),
            vmem((24, 128), F32),
            vmem((SUBSTEPS, 2, 56, 128), F32),
            vmem((SUBSTEPS, 4, 8, 128), F32),
            vmem((SUBSTEPS, 2, 24, 128), F32),
            vmem((SUBSTEPS, 2, 56, 128), F32),
            vmem((SUBSTEPS, 4, 8, 128), F32),
            vmem((SUBSTEPS, 2, 24, 128), F32),
            vmem((3, 64, 128), F32),
            vmem((3, 64, 128), F32),
            pltpu.SemaphoreType.DMA((9,)),
            pltpu.SemaphoreType.DMA((5,)),
            pltpu.SemaphoreType.DMA((5,)),
            pltpu.SemaphoreType.DMA((SUBSTEPS, 8)),
            pltpu.SemaphoreType.DMA((SUBSTEPS, 8)),
        ],
        compiler_params=pltpu.CompilerParams(collective_id=0, has_side_effects=True),
        name="substeps",
    )(
        displacement.reshape(3, 64, 128),
        velocity.reshape(3, 64, 128),
        inverse_mass.reshape(1, 64, 128),
        lame_first,
        lame_second,
        level_map,
        spread,
        gather,
        pack,
    )
    return uo.reshape(3, 4, 16, 128), vo.reshape(3, 4, 16, 128)


def solution(mesh):
    in_specs = (
        P(None, "px", "py", None),
        P(None, "px", "py", None),
        P("px", "py", None),
        P(None, None, None, "px", "py"),
        P(None, None, None, "px", "py"),
        P("px", "py"),
    )
    out_specs = (P(None, "px", "py", None), P(None, "px", "py", None))
    body = functools.partial(shards, mesh.shape["px"], mesh.shape["py"])
    return jax.shard_map(body, mesh=mesh, in_specs=in_specs, out_specs=out_specs, check_vma=False)
```

```python
import functools

import jax
import jax.numpy as jnp
import ml_dtypes
import numpy as np
from jax import lax
from jax.experimental import pallas as pl
from jax.experimental.pallas import tpu as pltpu
from jax.sharding import PartitionSpec as P

SUBSTEPS = 4
TIME_STEP = 0.1
MESH = pl.DeviceIdType.MESH
F32 = jnp.float32
BF16 = jnp.bfloat16
NEIGHBOURS = [(1, 0), (-1, 0), (1, 1), (1, -1), (-1, 1), (-1, -1), (0, 1), (0, -1)]
SLOT = {d: n for n, d in enumerate(NEIGHBOURS)}
XF, XB, DPP, DPM, DMP, DMM, YU, YD = range(8)


def gll_tables():
    points = np.array([-1.0, -np.sqrt(3.0 / 7.0), 0.0, np.sqrt(3.0 / 7.0), 1.0])
    weights = np.array([0.1, 49.0 / 90.0, 32.0 / 45.0, 49.0 / 90.0, 0.1])
    legendre = (35.0 * points**4 - 30.0 * points**2 + 3.0) / 8.0
    derivative = np.zeros((5, 5))
    for row in range(5):
        for col in range(5):
            if row != col:
                derivative[row, col] = legendre[row] / (legendre[col] * (points[row] - points[col]))
    derivative[0, 0] = -5.0
    derivative[4, 4] = 5.0
    return derivative, weights


def place(k, j):
    if k < 4 and j < 4:
        return k * 4 + j
    return 16 + k if k < 4 else 20 + j


@functools.cache
def tables():
    spread = np.zeros((512, 512), ml_dtypes.bfloat16)
    pack = np.zeros((128, 128), ml_dtypes.bfloat16)
    for k in range(4):
        for c in range(32):
            pack[4 * c + k, k * 32 + c] = 1
            for b in range(4):
                spread[b * 128 + 4 * c + k, k * 128 + b * 32 + c] = 1
    return spread, np.ascontiguousarray(spread.T), pack


def apply(matrix, v):
    even0, odd0 = v[0] + v[4], v[0] - v[4]
    even1, odd1 = v[1] + v[3], v[1] - v[3]
    out = [None] * 5
    for a in range(2):
        row = matrix[a]
        first = float(row[0] - row[4]) / 2 * odd0 + float(row[1] - row[3]) / 2 * odd1
        second = float(row[0] + row[4]) / 2 * even0 + float(row[1] + row[3]) / 2 * even1 + float(row[2]) * v[2]
        out[a], out[4 - a] = first + second, first - second
    out[2] = float(matrix[2][0]) * odd0 + float(matrix[2][1]) * odd1
    return out


def halves(value):
    high = value.astype(BF16)
    return high, (value - high.astype(F32)).astype(BF16)


def permute(value, matrix):
    high, low = halves(value)
    rows = value.shape[0]
    out = jnp.dot(jnp.concatenate([high, low], axis=0), matrix, preferred_element_type=F32)
    return out[:rows] + out[rows:]


def kernel(
    nx,
    ny,
    u_hbm,
    v_hbm,
    im_hbm,
    la_hbm,
    mu_hbm,
    level_hbm,
    spread_hbm,
    gather_hbm,
    pack_hbm,
    uo_vm,
    vo_vm,
    u_vm,
    vim_vm,
    la_raw,
    mu_raw,
    la_vm,
    mu_vm,
    mu_twice,
    level_vm,
    spread_vm,
    gather_vm,
    pack_vm,
    halo_u,
    halo_vim,
    halo_y_send,
    halo_y,
    halo_c_send,
    halo_c,
    x_own,
    x_line,
    u_all,
    v_own,
    im_own,
    u_line,
    v_line,
    im_line,
    grad_z,
    stress_x,
    f_new,
    f_kept,
    f_sum,
    pack_up,
    pack_down,
    send_x,
    send_d,
    send_y,
    recv_x,
    recv_d,
    recv_y,
    load_sem,
    halo_send_sem,
    halo_recv_sem,
    send_sem,
    recv_sem,
):
    px, py = lax.axis_index("px"), lax.axis_index("py")

    def present(dx, dy):
        conditions = []
        if dx:
            conditions.append(px < nx - 1 if dx > 0 else px > 0)
        if dy:
            conditions.append(py < ny - 1 if dy > 0 else py > 0)
        return functools.reduce(jnp.logical_and, conditions)

    barrier = pltpu.get_barrier_semaphore()
    for dx, dy in NEIGHBOURS:

        @pl.when(present(dx, dy))
        def _():
            pl.semaphore_signal(barrier, inc=1, device_id=(px + dx, py + dy), device_id_type=MESH)

    loads = []
    for n, (source, target) in enumerate(
        [
            (u_hbm, u_vm),
            (v_hbm, vim_vm.at[0:3]),
            (im_hbm, vim_vm.at[3:4]),
            (spread_hbm, spread_vm),
            (pack_hbm, pack_vm),
            (la_hbm, la_raw),
            (mu_hbm, mu_raw),
            (level_hbm, level_vm),
            (gather_hbm, gather_vm),
        ]
    ):
        loads.append(pltpu.make_async_copy(source, target, load_sem.at[n]))
        loads[-1].start()

    x_own[...] = jnp.zeros_like(x_own)
    x_line[...] = jnp.zeros_like(x_line)
    u_all[...] = jnp.zeros_like(u_all)

    for n, (dx, dy) in enumerate(NEIGHBOURS):

        @pl.when(jnp.logical_not(present(-dx, -dy)))
        def _():
            for s in range(SUBSTEPS):
                if n < 2:
                    recv_x[s, n] = jnp.zeros_like(recv_x[s, n])
                elif n < 6:
                    recv_d[s, n - 2] = jnp.zeros_like(recv_d[s, n - 2])
                else:
                    recv_y[s, n - 6] = jnp.zeros_like(recv_y[s, n - 6])
            if n == XB:
                halo_u[...] = jnp.zeros_like(halo_u)
                halo_vim[...] = jnp.zeros_like(halo_vim)
            if n == YD:
                halo_y[...] = jnp.zeros_like(halo_y)
            if n == DMM:
                halo_c[...] = jnp.zeros_like(halo_c)

    for n in range(3):
        loads[n].wait()
    for c in range(7):
        source = u_vm.at[c] if c < 3 else vim_vm.at[c - 3]
        halo_y_send[4 * c : 4 * c + 4, :] = source[pl.ds(0, 4, stride=16), :]
        halo_c_send[c : c + 1, :] = source[0:1, :]

    def remote(source, target, sems, n, dx, dy):
        send, recv = sems
        return pltpu.make_async_remote_copy(
            src_ref=source,
            dst_ref=target,
            send_sem=send.at[n],
            recv_sem=recv.at[n],
            device_id=(px + dx, py + dy),
            device_id_type=MESH,
        )

    halo_sems = (halo_send_sem, halo_recv_sem)
    halos = [
        remote(u_hbm.at[:, 0:16, :], halo_u, halo_sems, 0, -1, 0),
        remote(halo_c_send, halo_c, halo_sems, 1, -1, -1),
        remote(halo_y_send, halo_y, halo_sems, 2, 0, -1),
        remote(v_hbm.at[:, 0:16, :], halo_vim.at[0:3], halo_sems, 3, -1, 0),
        remote(im_hbm.at[:, 0:16, :], halo_vim.at[3:4], halo_sems, 4, -1, 0),
    ]
    halo_to = [(-1, 0), (-1, -1), (0, -1), (-1, 0), (-1, 0)]

    neighbours = 0
    for dx, dy in NEIGHBOURS:
        neighbours = neighbours + present(dx, dy).astype(jnp.int32)
    pl.semaphore_wait(barrier, neighbours)
    for copy, to in zip(halos, halo_to):

        @pl.when(present(*to))
        def _():
            copy.start()

    def wait_halo(n):
        dx, dy = halo_to[n]

        @pl.when(present(-dx, -dy))
        def _():
            halos[n].wait_recv()

    lane = lax.broadcasted_iota(jnp.int32, (8, 128), 1)
    sublane = lax.broadcasted_iota(jnp.int32, (8, 128), 0)
    depth = lane & 31
    column = lane >> 5

    def fill_own(c, source):
        for j in range(4):
            for b in range(4):
                row = (c * 4 + j) * 8
                x_own[b, row : row + 4, :] = source[pl.ds(4 * b + j, 4, stride=16), :]

    def fill_far(c, source):
        for b in range(4):
            x_own[b, pl.ds(c * 32 + 4, 4, stride=8), :] = source[4 * b : 4 * b + 4, :]

    def spread(first_row, rows):
        wide = jnp.concatenate([x_own[b, first_row : first_row + rows, :] for b in range(4)], axis=1)
        return permute(wide, spread_vm[...])

    for c in range(3):
        fill_own(c, u_vm.at[c])
    for c in range(4):
        fill_own(3 + c, vim_vm.at[c])
    loads[3].wait()
    loads[4].wait()
    for n in range(5, 9):
        loads[n].wait()
    derivative, weights = gll_tables()
    la_vm[...] = jnp.zeros_like(la_vm)
    mu_vm[...] = jnp.zeros_like(mu_vm)
    for k in range(5):
        for j in range(5):
            for i in range(5):
                weight = float(weights[i] * weights[j] * weights[k])
                row = (k * 5 + j) * 8 + i
                la_vm[row : row + 1, :] = weight * la_raw[i, j, k]
                mu_vm[row : row + 1, :] = weight * mu_raw[i, j, k]
    mu_twice[...] = 2.0 * mu_vm[...]

    wait_halo(0)
    wait_halo(1)
    wait_halo(2)
    for c in range(3):
        fill_far(c, halo_u.at[c])
    for c in range(7):
        x_line[c * 8 : c * 8 + 4, :] = halo_y[4 * c : 4 * c + 4, :]
        x_line[c * 8 + 4 : c * 8 + 5, :] = halo_c[c : c + 1, :]
    nodes = spread(0, 96)
    for c in range(3):
        for j in range(4):
            for k in range(4):
                row = (c * 4 + j) * 8
                u_all[c, (k * 4 + j) * 8 : (k * 4 + j + 1) * 8, :] = nodes[row : row + 8, k * 128 : (k + 1) * 128]
    lines = permute(x_line[...], pack_vm[...])
    u_line[...] = lines[0:24]
    v_line[...] = lines[24:48]
    im_line[...] = TIME_STEP * lines[48:56]

    def group(p):
        return pl.ds(p * 8, 8)

    def expand():
        for c in range(3):
            line = u_line[c * 8 : c * 8 + 8, :]
            for k in range(4):
                inner = pltpu.roll(u_all[c, group(k * 4), :], 96, 1)
                outer = pltpu.roll(line, (96 - 32 * k) % 128, 1) if k != 3 else line
                u_all[c, group(16 + k), :] = jnp.where(column == 3, outer, inner)
            for j in range(5):
                below = pltpu.roll(u_all[c, group(j if j < 4 else 16), :], 127, 1)
                u_all[c, group(20 + j), :] = jnp.where(depth < 31, below, 0.0)

    def columns(matrix):
        out = []
        for n in range(5):
            values = jnp.zeros((8, 128), F32)
            for i in range(5):
                values = jnp.where(sublane == i, float(matrix[i][n]), values)
            out.append(values)
        return out

    def along_x(vectors, ref, c, row):
        total = vectors[0] * jnp.broadcast_to(ref[c, row : row + 1, :], (8, 128))
        for n in range(1, 5):
            total = total + vectors[n] * jnp.broadcast_to(ref[c, row + n : row + n + 1, :], (8, 128))
        return total

    def forces(s):
        forward, backward = columns(derivative), columns(derivative.T)
        for c in range(3):
            for j in range(5):
                out = apply(derivative, [u_all[c, group(place(k, j)), :] for k in range(5)])
                for k in range(5):
                    grad_z[c, group(k * 5 + j), :] = out[k]
        for k in range(5):
            gy = [apply(derivative, [u_all[c, group(place(k, j)), :] for j in range(5)]) for c in range(3)]
            stress_y = [[], [], []]
            for j in range(5):
                rows = group(k * 5 + j)
                gx = [along_x(forward, u_all, c, place(k, j) * 8) for c in range(3)]
                gz = [grad_z[c, rows, :] for c in range(3)]
                first, second, twice = la_vm[rows, :], mu_vm[rows, :], mu_twice[rows, :]
                pressure = first * (gx[0] + gy[1][j] + gz[2])
                xy = second * (gy[0][j] + gx[1])
                xz = second * (gz[0] + gx[2])
                yz = second * (gz[1] + gy[2][j])
                stress_x[0, rows, :] = pressure + twice * gx[0]
                stress_x[1, rows, :] = xy
                stress_x[2, rows, :] = xz
                stress_y[0].append(xy)
                stress_y[1].append(pressure + twice * gy[1][j])
                stress_y[2].append(yz)
                grad_z[0, rows, :] = xz
                grad_z[1, rows, :] = yz
                grad_z[2, rows, :] = pressure + twice * gz[2]
            for c in range(3):
                out = apply(derivative.T, stress_y[c])
                for j in range(5):
                    f_new[c, group(k * 5 + j), :] = out[j] + along_x(backward, stress_x, c, (k * 5 + j) * 8)
        least = jnp.where(s == 0, 0, jnp.where(s == 2, 1, 2))
        active = jnp.broadcast_to(level_vm[...], (8, 128)) >= least
        for c in range(3):
            for j in range(5):
                out = apply(derivative.T, [grad_z[c, group(k * 5 + j), :] for k in range(5)])
                for k in range(5):
                    new = f_new[c, group(k * 5 + j), :] + out[k]
                    rows = group(place(k, j))
                    f_kept[c, rows, :] = jnp.where(active, new, f_kept[c, rows, :])

    def assemble(s, last):
        for c in range(3):
            f = [f_kept[c, group(p), :] for p in range(25)]
            for j in range(5):
                p = j if j < 4 else 16
                f[p] = f[p] + jnp.where(depth > 0, pltpu.roll(f[20 + j], 1, 1), 0.0)
            up = jnp.zeros((8, 128), F32)
            down = jnp.zeros((8, 128), F32)
            for k in range(4):
                shifted = pltpu.roll(f[16 + k], 32, 1)
                up = jnp.where(column == k, pltpu.roll(shifted, 32 * k, 1) if k else shifted, up)
                down = jnp.where(column == k, pltpu.roll(f[4 * k], 32 * k, 1) if k else f[0], down)
                f[4 * k] = f[4 * k] + jnp.where(column > 0, shifted, 0.0)
            for p in range(16):
                f_sum[c, group(p), :] = f[p]
            pack_up[c * 8 : c * 8 + 8, :] = up
            pack_down[c * 8 : c * 8 + 8, :] = down
        for c in range(3):
            send_x[s, XF, c * 16 : c * 16 + 16, :] = f_sum[c, pl.ds(4, 16, stride=8), :]
            if not last:
                send_x[s, XB, c * 16 : c * 16 + 16, :] = f_sum[c, pl.ds(0, 16, stride=8), :]
        up_far = pack_up[pl.ds(4, 3, stride=8), :]
        send_d[s, DPP - 2, 0:3, :] = up_far
        send_y[s, 0] = pack_up[...]
        if not last:
            up_near = pack_up[pl.ds(0, 3, stride=8), :]
            send_d[s, DPM - 2, 0:3, :] = pack_down[pl.ds(4, 3, stride=8), :]
            send_d[s, DMP - 2, 0:3, :] = up_near
            send_d[s, DMM - 2, 0:3, :] = pack_down[pl.ds(0, 3, stride=8), :]
            send_x[s, XF, 48:51, :] = up_far
            send_x[s, XB, 48:51, :] = up_near
            send_y[s, 1] = pack_down[...]

    def exchange(s, last):
        copies = []
        for n, (dx, dy) in enumerate(NEIGHBOURS):
            if last and (dx < 0 or dy < 0):
                continue
            if n < 2:
                pair = (send_x.at[s, n], recv_x.at[s, n])
            elif n < 6:
                pair = (send_d.at[s, n - 2], recv_d.at[s, n - 2])
            else:
                pair = (send_y.at[s, n - 6], recv_y.at[s, n - 6])
            copies.append(((dx, dy), remote(*pair, (send_sem.at[s], recv_sem.at[s]), n, dx, dy)))
        return copies

    def start(copies):
        for to, copy in copies:

            @pl.when(present(*to))
            def _():
                copy.start()

    def arrive(copies):
        for (dx, dy), copy in copies:

            @pl.when(present(-dx, -dy))
            def _():
                copy.wait_recv()

    def finish(copies):
        for to, copy in copies:

            @pl.when(present(*to))
            def _():
                copy.wait_send()

    def advance(s, last):
        for c in range(3):
            near = recv_y[s, 0, c * 8 : c * 8 + 8, :]
            near = near + jnp.where(sublane == 0, recv_d[s, DPP - 2, c : c + 1, :], 0.0)
            if not last:
                near = near + jnp.where(sublane == 4, recv_d[s, DMP - 2, c : c + 1, :], 0.0)
            for k in range(4):
                part = pltpu.roll(near, 128 - 32 * k, 1) if k else near
                f_sum[c, group(4 * k), :] = f_sum[c, group(4 * k), :] + jnp.where(column == 0, part, 0.0)
            f_sum[c, pl.ds(0, 16, stride=8), :] = f_sum[c, pl.ds(0, 16, stride=8), :] + recv_x[s, XF, c * 16 : c * 16 + 16, :]
            if not last:
                f_sum[c, pl.ds(4, 16, stride=8), :] = (
                    f_sum[c, pl.ds(4, 16, stride=8), :] + recv_x[s, XB, c * 16 : c * 16 + 16, :]
                )
        for c in range(3):
            v = v_own[c] - im_own[...] * f_sum[c]
            v_own[c] = v
            u_all[c, 0:128, :] = u_all[c, 0:128, :] + TIME_STEP * v
        if last:
            return
        for c in range(3):
            rows = slice(c * 8, c * 8 + 8)
            far = pack_up[rows, :] + recv_y[s, 1, rows, :]
            left = recv_x[s, XF, 48 + c : 49 + c, :] + recv_d[s, DPM - 2, c : c + 1, :]
            right = recv_x[s, XB, 48 + c : 49 + c, :] + recv_d[s, DMM - 2, c : c + 1, :]
            far = far + jnp.where(sublane == 0, left, 0.0) + jnp.where(sublane == 4, right, 0.0)
            v = v_line[rows, :] - im_line[...] * far
            v_line[rows, :] = v
            u_line[rows, :] = u_line[rows, :] + TIME_STEP * v
        expand()

    def late_nodes():
        wait_halo(3)
        wait_halo(4)
        for c in range(4):
            fill_far(3 + c, halo_vim.at[c])
        values = spread(96, 128)
        for c in range(4):
            for j in range(4):
                for k in range(4):
                    row = (c * 4 + j) * 8
                    value = values[row : row + 8, k * 128 : (k + 1) * 128]
                    if c < 3:
                        v_own[c, group(k * 4 + j), :] = value
                    else:
                        im_own[group(k * 4 + j), :] = TIME_STEP * value

    expand()
    forces(0)
    assemble(0, False)
    copies = exchange(0, False)
    start(copies)
    late_nodes()
    arrive(copies)
    advance(0, False)

    def substep(s, carry):
        forces(s)
        assemble(s, False)
        copies = exchange(s, False)
        start(copies)
        arrive(copies)
        advance(s, False)
        return carry

    lax.fori_loop(1, SUBSTEPS - 1, substep, 0)
    s = SUBSTEPS - 1
    forces(s)
    assemble(s, True)
    copies = exchange(s, True)
    start(copies)
    arrive(copies)
    advance(s, True)

    rows = []
    for source in (u_all, v_own):
        for c in range(3):
            for j in range(4):
                rows.append(jnp.concatenate([source[c, group(k * 4 + j), :] for k in range(4)], axis=1))
    result = permute(jnp.concatenate(rows, axis=0), gather_vm[...])
    for a, target in enumerate((uo_vm, vo_vm)):
        for c in range(3):
            for j in range(4):
                row = ((a * 3 + c) * 4 + j) * 8
                for b in range(4):
                    target[c, pl.ds(4 * b + j, 4, stride=16), :] = result[row : row + 4, b * 128 : (b + 1) * 128]
    for copy, to in zip(halos, halo_to):

        @pl.when(present(*to))
        def _():
            copy.wait_send()

    def drain(s, carry):
        finish(exchange(s, False))
        return carry

    lax.fori_loop(0, SUBSTEPS - 1, drain, 0)
    finish(exchange(SUBSTEPS - 1, True))


def write_out(u_ref, v_ref, uo_ref, vo_ref, sem):
    copies = [
        pltpu.make_async_copy(u_ref, uo_ref, sem.at[0]),
        pltpu.make_async_copy(v_ref, vo_ref, sem.at[1]),
    ]
    for copy in copies:
        copy.start()
    for copy in copies:
        copy.wait()


def shards(nx, ny, displacement, velocity, inverse_mass, lame_first, lame_second, level_map):
    spread, gather, pack = (jnp.asarray(table) for table in tables())
    vmem = pltpu.VMEM
    uo, vo = pl.pallas_call(
        functools.partial(kernel, nx, ny),
        out_shape=[jax.ShapeDtypeStruct((3, 64, 128), F32)] * 2,
        in_specs=[pl.BlockSpec(memory_space=pltpu.HBM)] * 9,
        out_specs=[pl.BlockSpec(memory_space=pltpu.VMEM)] * 2,
        scratch_shapes=[
            vmem((3, 64, 128), F32),
            vmem((4, 64, 128), F32),
            vmem((5, 5, 5, 1, 128), F32),
            vmem((5, 5, 5, 1, 128), F32),
            vmem((200, 128), F32),
            vmem((200, 128), F32),
            vmem((200, 128), F32),
            vmem((1, 128), jnp.int32),
            vmem((512, 512), BF16),
            vmem((512, 512), BF16),
            vmem((128, 128), BF16),
            vmem((3, 16, 128), F32),
            vmem((4, 16, 128), F32),
            vmem((32, 128), F32),
            vmem((32, 128), F32),
            vmem((8, 128), F32),
            vmem((8, 128), F32),
            vmem((4, 224, 128), F32),
            vmem((56, 128), F32),
            vmem((3, 200, 128), F32),
            vmem((3, 128, 128), F32),
            vmem((128, 128), F32),
            vmem((24, 128), F32),
            vmem((24, 128), F32),
            vmem((8, 128), F32),
            vmem((3, 200, 128), F32),
            vmem((3, 200, 128), F32),
            vmem((3, 200, 128), F32),
            vmem((3, 200, 128), F32),
            vmem((3, 128, 128), F32),
            vmem((24, 128), F32),
            vmem((24, 128), F32),
            vmem((SUBSTEPS, 2, 56, 128), F32),
            vmem((SUBSTEPS, 4, 8, 128), F32),
            vmem((SUBSTEPS, 2, 24, 128), F32),
            vmem((SUBSTEPS, 2, 56, 128), F32),
            vmem((SUBSTEPS, 4, 8, 128), F32),
            vmem((SUBSTEPS, 2, 24, 128), F32),
            pltpu.SemaphoreType.DMA((9,)),
            pltpu.SemaphoreType.DMA((5,)),
            pltpu.SemaphoreType.DMA((5,)),
            pltpu.SemaphoreType.DMA((SUBSTEPS, 8)),
            pltpu.SemaphoreType.DMA((SUBSTEPS, 8)),
        ],
        compiler_params=pltpu.CompilerParams(collective_id=0, has_side_effects=True, vmem_limit_bytes=16 * 2**20),
        name="substeps",
    )(
        *(
            pltpu.with_memory_space_constraint(array, pltpu.HBM)
            for array in (
                displacement.reshape(3, 64, 128),
                velocity.reshape(3, 64, 128),
                inverse_mass.reshape(1, 64, 128),
                lame_first,
                lame_second,
                level_map,
                spread,
                gather,
                pack,
            )
        )
    )
    uo, vo = pl.pallas_call(
        write_out,
        out_shape=[jax.ShapeDtypeStruct((3, 64, 128), F32)] * 2,
        in_specs=[pl.BlockSpec(memory_space=pl.ANY)] * 2,
        out_specs=[pl.BlockSpec(memory_space=pl.ANY)] * 2,
        scratch_shapes=[pltpu.SemaphoreType.DMA((2,))],
        compiler_params=pltpu.CompilerParams(vmem_limit_bytes=2**20),
        name="write_out",
    )(uo, vo)
    return uo.reshape(3, 4, 16, 128), vo.reshape(3, 4, 16, 128)


def solution(mesh):
    in_specs = (
        P(None, "px", "py", None),
        P(None, "px", "py", None),
        P("px", "py", None),
        P(None, None, None, "px", "py"),
        P(None, None, None, "px", "py"),
        P("px", "py"),
    )
    out_specs = (P(None, "px", "py", None), P(None, "px", "py", None))
    body = functools.partial(shards, mesh.shape["px"], mesh.shape["py"])
    return jax.shard_map(body, mesh=mesh, in_specs=in_specs, out_specs=out_specs, check_vma=False)
```

```python
import functools

import jax
import jax.numpy as jnp
import ml_dtypes
import numpy as np
from jax import lax
from jax.experimental import pallas as pl
from jax.experimental.pallas import tpu as pltpu
from jax.sharding import PartitionSpec as P

SUBSTEPS = 4
TIME_STEP = 0.1
MESH = pl.DeviceIdType.MESH
F32 = jnp.float32
BF16 = jnp.bfloat16
NEIGHBOURS = [(1, 0), (-1, 0), (1, 1), (1, -1), (-1, 1), (-1, -1), (0, 1), (0, -1)]
SLOT = {d: n for n, d in enumerate(NEIGHBOURS)}
XF, XB, DPP, DPM, DMP, DMM, YU, YD = range(8)


def gll_tables():
    points = np.array([-1.0, -np.sqrt(3.0 / 7.0), 0.0, np.sqrt(3.0 / 7.0), 1.0])
    weights = np.array([0.1, 49.0 / 90.0, 32.0 / 45.0, 49.0 / 90.0, 0.1])
    legendre = (35.0 * points**4 - 30.0 * points**2 + 3.0) / 8.0
    derivative = np.zeros((5, 5))
    for row in range(5):
        for col in range(5):
            if row != col:
                derivative[row, col] = legendre[row] / (legendre[col] * (points[row] - points[col]))
    derivative[0, 0] = -5.0
    derivative[4, 4] = 5.0
    return derivative, weights


def place(k, j):
    if k < 4 and j < 4:
        return k * 4 + j
    return 16 + k if k < 4 else 20 + j


@functools.cache
def tables():
    spread = np.zeros((512, 512), ml_dtypes.bfloat16)
    pack = np.zeros((128, 128), ml_dtypes.bfloat16)
    for k in range(4):
        for c in range(32):
            pack[4 * c + k, k * 32 + c] = 1
            for b in range(4):
                spread[b * 128 + 4 * c + k, k * 128 + b * 32 + c] = 1
    return spread, np.ascontiguousarray(spread.T), pack


def apply(matrix, v):
    even0, odd0 = v[0] + v[4], v[0] - v[4]
    even1, odd1 = v[1] + v[3], v[1] - v[3]
    out = [None] * 5
    for a in range(2):
        row = matrix[a]
        first = float(row[0] - row[4]) / 2 * odd0 + float(row[1] - row[3]) / 2 * odd1
        second = float(row[0] + row[4]) / 2 * even0 + float(row[1] + row[3]) / 2 * even1 + float(row[2]) * v[2]
        out[a], out[4 - a] = first + second, first - second
    out[2] = float(matrix[2][0]) * odd0 + float(matrix[2][1]) * odd1
    return out


def halves(value):
    high = value.astype(BF16)
    return high, (value - high.astype(F32)).astype(BF16)


def permute(value, matrix):
    high, low = halves(value)
    rows = value.shape[0]
    out = jnp.dot(jnp.concatenate([high, low], axis=0), matrix, preferred_element_type=F32)
    return out[:rows] + out[rows:]


def kernel(
    nx,
    ny,
    u_hbm,
    v_hbm,
    im_hbm,
    la_hbm,
    mu_hbm,
    level_hbm,
    spread_hbm,
    gather_hbm,
    pack_hbm,
    uo_vm,
    vo_vm,
    u_vm,
    vim_vm,
    la_raw,
    mu_raw,
    la_vm,
    mu_vm,
    mu_twice,
    level_vm,
    spread_vm,
    gather_vm,
    pack_vm,
    halo_u,
    halo_vim,
    halo_y_send,
    halo_y,
    halo_c_send,
    halo_c,
    x_own,
    x_face,
    x_line,
    u_all,
    v_own,
    im_own,
    u_line,
    v_line,
    im_line,
    grad_z,
    stress_x,
    f_new,
    f_kept,
    f_sum,
    pack_up,
    pack_down,
    send_x,
    send_d,
    send_y,
    recv_x,
    recv_d,
    recv_y,
    load_sem,
    halo_send_sem,
    halo_recv_sem,
    send_sem,
    recv_sem,
):
    px, py = lax.axis_index("px"), lax.axis_index("py")

    def present(dx, dy):
        conditions = []
        if dx:
            conditions.append(px < nx - 1 if dx > 0 else px > 0)
        if dy:
            conditions.append(py < ny - 1 if dy > 0 else py > 0)
        return functools.reduce(jnp.logical_and, conditions)

    barrier = pltpu.get_barrier_semaphore()
    for dx, dy in NEIGHBOURS:

        @pl.when(present(dx, dy))
        def _():
            pl.semaphore_signal(barrier, inc=1, device_id=(px + dx, py + dy), device_id_type=MESH)

    loads = []
    for n, (source, target) in enumerate(
        [
            (u_hbm, u_vm),
            (v_hbm, vim_vm.at[0:3]),
            (im_hbm, vim_vm.at[3:4]),
            (spread_hbm, spread_vm),
            (pack_hbm, pack_vm),
            (la_hbm, la_raw),
            (mu_hbm, mu_raw),
            (level_hbm, level_vm),
            (gather_hbm, gather_vm),
        ]
    ):
        loads.append(pltpu.make_async_copy(source, target, load_sem.at[n]))
        loads[-1].start()

    x_own[...] = jnp.zeros_like(x_own)
    x_line[...] = jnp.zeros_like(x_line)
    x_face[...] = jnp.zeros_like(x_face)
    u_all[...] = jnp.zeros_like(u_all)

    for n, (dx, dy) in enumerate(NEIGHBOURS):

        @pl.when(jnp.logical_not(present(-dx, -dy)))
        def _():
            for s in range(SUBSTEPS):
                if n < 2:
                    recv_x[s, n] = jnp.zeros_like(recv_x[s, n])
                elif n < 6:
                    recv_d[s, n - 2] = jnp.zeros_like(recv_d[s, n - 2])
                else:
                    recv_y[s, n - 6] = jnp.zeros_like(recv_y[s, n - 6])
            if n == XB:
                halo_u[...] = jnp.zeros_like(halo_u)
                halo_vim[...] = jnp.zeros_like(halo_vim)
            if n == YD:
                halo_y[...] = jnp.zeros_like(halo_y)
            if n == DMM:
                halo_c[...] = jnp.zeros_like(halo_c)

    for n in range(3):
        loads[n].wait()
    for c in range(7):
        source = u_vm.at[c] if c < 3 else vim_vm.at[c - 3]
        halo_y_send[4 * c : 4 * c + 4, :] = source[pl.ds(0, 4, stride=16), :]
        halo_c_send[c : c + 1, :] = source[0:1, :]

    def remote(source, target, sems, n, dx, dy):
        send, recv = sems
        return pltpu.make_async_remote_copy(
            src_ref=source,
            dst_ref=target,
            send_sem=send.at[n],
            recv_sem=recv.at[n],
            device_id=(px + dx, py + dy),
            device_id_type=MESH,
        )

    halo_sems = (halo_send_sem, halo_recv_sem)
    halos = [
        remote(u_hbm.at[:, 0:16, :], halo_u, halo_sems, 0, -1, 0),
        remote(halo_c_send, halo_c, halo_sems, 1, -1, -1),
        remote(halo_y_send, halo_y, halo_sems, 2, 0, -1),
        remote(v_hbm.at[:, 0:16, :], halo_vim.at[0:3], halo_sems, 3, -1, 0),
        remote(im_hbm.at[:, 0:16, :], halo_vim.at[3:4], halo_sems, 4, -1, 0),
    ]
    halo_to = [(-1, 0), (-1, -1), (0, -1), (-1, 0), (-1, 0)]

    neighbours = 0
    for dx, dy in NEIGHBOURS:
        neighbours = neighbours + present(dx, dy).astype(jnp.int32)
    pl.semaphore_wait(barrier, neighbours)
    for copy, to in zip(halos, halo_to):

        @pl.when(present(*to))
        def _():
            copy.start()

    def wait_halo(n):
        dx, dy = halo_to[n]

        @pl.when(present(-dx, -dy))
        def _():
            halos[n].wait_recv()

    lane = lax.broadcasted_iota(jnp.int32, (8, 128), 1)
    sublane = lax.broadcasted_iota(jnp.int32, (8, 128), 0)
    depth = lane & 31
    column = lane >> 5

    def fill_own(c, source):
        for j in range(4):
            for b in range(4):
                row = (c * 4 + j) * 8
                x_own[b, row : row + 4, :] = source[pl.ds(4 * b + j, 4, stride=16), :]

    def wide(ref, first_row, rows):
        return jnp.concatenate([ref[b, first_row : first_row + rows, :] for b in range(4)], axis=1)

    def far_rows(source, count):
        for c in range(count):
            for b in range(4):
                x_face[b, c * 4 : c * 4 + 4, :] = source[c, 4 * b : 4 * b + 4, :]
        return permute(wide(x_face, 0, 16), spread_vm[...])

    for c in range(3):
        fill_own(c, u_vm.at[c])
    for c in range(4):
        fill_own(3 + c, vim_vm.at[c])
    loads[3].wait()
    loads[4].wait()
    for n in range(5, 9):
        loads[n].wait()
    derivative, weights = gll_tables()
    la_vm[...] = jnp.zeros_like(la_vm)
    mu_vm[...] = jnp.zeros_like(mu_vm)
    for k in range(5):
        for j in range(5):
            for i in range(5):
                weight = float(weights[i] * weights[j] * weights[k])
                row = (k * 5 + j) * 8 + i
                la_vm[row : row + 1, :] = weight * la_raw[i, j, k]
                mu_vm[row : row + 1, :] = weight * mu_raw[i, j, k]
    mu_twice[...] = 2.0 * mu_vm[...]

    nodes = permute(wide(x_own, 0, 224), spread_vm[...])
    for c in range(7):
        for j in range(4):
            for k in range(4):
                row = (c * 4 + j) * 8
                rows = pl.ds((k * 4 + j) * 8, 8)
                value = nodes[row : row + 8, k * 128 : (k + 1) * 128]
                if c < 3:
                    u_all[c, rows, :] = value
                elif c < 6:
                    v_own[c - 3, rows, :] = value
                else:
                    im_own[rows, :] = TIME_STEP * value

    wait_halo(2)
    for c in range(7):
        x_line[c * 8 : c * 8 + 4, :] = halo_y[4 * c : 4 * c + 4, :]
    wait_halo(0)
    wait_halo(1)
    face = far_rows(halo_u, 3)
    for c in range(3):
        for k in range(4):
            u_all[c, pl.ds(k * 32 + 4, 4, stride=8), :] = face[c * 4 : c * 4 + 4, k * 128 : (k + 1) * 128]
    for c in range(7):
        x_line[c * 8 + 4 : c * 8 + 5, :] = halo_c[c : c + 1, :]
    u_line[...] = permute(x_line[0:24, :], pack_vm[...])

    def group(p):
        return pl.ds(p * 8, 8)

    def expand():
        for c in range(3):
            line = u_line[c * 8 : c * 8 + 8, :]
            for k in range(4):
                inner = pltpu.roll(u_all[c, group(k * 4), :], 96, 1)
                outer = pltpu.roll(line, (96 - 32 * k) % 128, 1) if k != 3 else line
                u_all[c, group(16 + k), :] = jnp.where(column == 3, outer, inner)
            for j in range(5):
                below = pltpu.roll(u_all[c, group(j if j < 4 else 16), :], 127, 1)
                u_all[c, group(20 + j), :] = jnp.where(depth < 31, below, 0.0)

    def columns(matrix):
        out = []
        for n in range(5):
            values = jnp.zeros((8, 128), F32)
            for i in range(5):
                values = jnp.where(sublane == i, float(matrix[i][n]), values)
            out.append(values)
        return out

    def along_x(vectors, ref, c, row):
        total = vectors[0] * jnp.broadcast_to(ref[c, row : row + 1, :], (8, 128))
        for n in range(1, 5):
            total = total + vectors[n] * jnp.broadcast_to(ref[c, row + n : row + n + 1, :], (8, 128))
        return total

    def forces(s):
        forward, backward = columns(derivative), columns(derivative.T)
        for c in range(3):
            for j in range(5):
                out = apply(derivative, [u_all[c, group(place(k, j)), :] for k in range(5)])
                for k in range(5):
                    grad_z[c, group(k * 5 + j), :] = out[k]
        for k in range(5):
            gy = [apply(derivative, [u_all[c, group(place(k, j)), :] for j in range(5)]) for c in range(3)]
            stress_y = [[], [], []]
            for j in range(5):
                rows = group(k * 5 + j)
                gx = [along_x(forward, u_all, c, place(k, j) * 8) for c in range(3)]
                gz = [grad_z[c, rows, :] for c in range(3)]
                first, second, twice = la_vm[rows, :], mu_vm[rows, :], mu_twice[rows, :]
                pressure = first * (gx[0] + gy[1][j] + gz[2])
                xy = second * (gy[0][j] + gx[1])
                xz = second * (gz[0] + gx[2])
                yz = second * (gz[1] + gy[2][j])
                stress_x[0, rows, :] = pressure + twice * gx[0]
                stress_x[1, rows, :] = xy
                stress_x[2, rows, :] = xz
                stress_y[0].append(xy)
                stress_y[1].append(pressure + twice * gy[1][j])
                stress_y[2].append(yz)
                grad_z[0, rows, :] = xz
                grad_z[1, rows, :] = yz
                grad_z[2, rows, :] = pressure + twice * gz[2]
            for c in range(3):
                out = apply(derivative.T, stress_y[c])
                for j in range(5):
                    f_new[c, group(k * 5 + j), :] = out[j] + along_x(backward, stress_x, c, (k * 5 + j) * 8)
        least = jnp.where(s == 0, 0, jnp.where(s == 2, 1, 2))
        active = jnp.broadcast_to(level_vm[...], (8, 128)) >= least
        for c in range(3):
            for j in range(5):
                out = apply(derivative.T, [grad_z[c, group(k * 5 + j), :] for k in range(5)])
                for k in range(5):
                    new = f_new[c, group(k * 5 + j), :] + out[k]
                    rows = group(place(k, j))
                    f_kept[c, rows, :] = jnp.where(active, new, f_kept[c, rows, :])

    def assemble(s, last):
        for c in range(3):
            f = [f_kept[c, group(p), :] for p in range(25)]
            for j in range(5):
                p = j if j < 4 else 16
                f[p] = f[p] + jnp.where(depth > 0, pltpu.roll(f[20 + j], 1, 1), 0.0)
            up = jnp.zeros((8, 128), F32)
            down = jnp.zeros((8, 128), F32)
            for k in range(4):
                shifted = pltpu.roll(f[16 + k], 32, 1)
                up = jnp.where(column == k, pltpu.roll(shifted, 32 * k, 1) if k else shifted, up)
                down = jnp.where(column == k, pltpu.roll(f[4 * k], 32 * k, 1) if k else f[0], down)
                f[4 * k] = f[4 * k] + jnp.where(column > 0, shifted, 0.0)
            for p in range(16):
                f_sum[c, group(p), :] = f[p]
            pack_up[c * 8 : c * 8 + 8, :] = up
            pack_down[c * 8 : c * 8 + 8, :] = down
        for c in range(3):
            send_x[s, XF, c * 16 : c * 16 + 16, :] = f_sum[c, pl.ds(4, 16, stride=8), :]
            if not last:
                send_x[s, XB, c * 16 : c * 16 + 16, :] = f_sum[c, pl.ds(0, 16, stride=8), :]
        up_far = pack_up[pl.ds(4, 3, stride=8), :]
        send_d[s, DPP - 2, 0:3, :] = up_far
        send_y[s, 0] = pack_up[...]
        if not last:
            up_near = pack_up[pl.ds(0, 3, stride=8), :]
            send_d[s, DPM - 2, 0:3, :] = pack_down[pl.ds(4, 3, stride=8), :]
            send_d[s, DMP - 2, 0:3, :] = up_near
            send_d[s, DMM - 2, 0:3, :] = pack_down[pl.ds(0, 3, stride=8), :]
            send_x[s, XF, 48:51, :] = up_far
            send_x[s, XB, 48:51, :] = up_near
            send_y[s, 1] = pack_down[...]

    def exchange(s, last):
        copies = []
        for n, (dx, dy) in enumerate(NEIGHBOURS):
            if last and (dx < 0 or dy < 0):
                continue
            if n < 2:
                pair = (send_x.at[s, n], recv_x.at[s, n])
            elif n < 6:
                pair = (send_d.at[s, n - 2], recv_d.at[s, n - 2])
            else:
                pair = (send_y.at[s, n - 6], recv_y.at[s, n - 6])
            copies.append(((dx, dy), remote(*pair, (send_sem.at[s], recv_sem.at[s]), n, dx, dy)))
        return copies

    def start(copies):
        for to, copy in copies:

            @pl.when(present(*to))
            def _():
                copy.start()

    def arrive(copies):
        for (dx, dy), copy in copies:

            @pl.when(present(-dx, -dy))
            def _():
                copy.wait_recv()

    def finish(copies):
        for to, copy in copies:

            @pl.when(present(*to))
            def _():
                copy.wait_send()

    def before_x(s, last):
        for c in range(3):
            rows = slice(c * 8, c * 8 + 8)
            near = recv_y[s, 0, rows, :]
            for k in range(4):
                part = pltpu.roll(near, 128 - 32 * k, 1) if k else near
                f_sum[c, group(4 * k), :] = f_sum[c, group(4 * k), :] + jnp.where(column == 0, part, 0.0)
            v = v_own[c] - im_own[...] * f_sum[c]
            v_own[c] = v
            u_all[c, 0:128, :] = u_all[c, 0:128, :] + TIME_STEP * v
            if not last:
                v = v_line[rows, :] - im_line[...] * (pack_up[rows, :] + recv_y[s, 1, rows, :])
                v_line[rows, :] = v
                u_line[rows, :] = u_line[rows, :] + TIME_STEP * v

    def with_corner(s, n, corner):
        for k in range(4):
            value = recv_d[s, corner - 2]
            part = pltpu.roll(value, 128 - 32 * k, 1) if k else value
            rows = pl.ds(4 * k, 3, stride=16)
            recv_x[s, n, rows, :] = recv_x[s, n, rows, :] + jnp.where(column == 0, part, 0.0)[0:3]

    def after_x(s):
        for n, corner, i in ((XF, DPP, 0), (XB, DMP, 4)):
            with_corner(s, n, corner)
            rows = pl.ds(i, 16, stride=8)
            scale = im_own[rows, :]
            for c in range(3):
                change = scale * recv_x[s, n, c * 16 : c * 16 + 16, :]
                v_own[c, rows, :] = v_own[c, rows, :] - change
                u_all[c, rows, :] = u_all[c, rows, :] - TIME_STEP * change
        for c in range(3):
            rows = slice(c * 8, c * 8 + 8)
            left = recv_x[s, XF, 48 + c : 49 + c, :] + recv_d[s, DPM - 2, c : c + 1, :]
            right = recv_x[s, XB, 48 + c : 49 + c, :] + recv_d[s, DMM - 2, c : c + 1, :]
            far = jnp.where(sublane == 0, left, jnp.where(sublane == 4, right, 0.0))
            change = im_line[...] * far
            v_line[rows, :] = v_line[rows, :] - change
            u_line[rows, :] = u_line[rows, :] - TIME_STEP * change
        expand()

    def late_nodes():
        v_line[...] = permute(x_line[24:48, :], pack_vm[...])
        im_line[...] = TIME_STEP * permute(x_line[48:56, :], pack_vm[...])
        wait_halo(3)
        wait_halo(4)
        face = far_rows(halo_vim, 4)
        for c in range(4):
            for k in range(4):
                rows = pl.ds(k * 32 + 4, 4, stride=8)
                value = face[c * 4 : c * 4 + 4, k * 128 : (k + 1) * 128]
                if c < 3:
                    v_own[c, rows, :] = value
                else:
                    im_own[rows, :] = TIME_STEP * value

    expand()
    forces(0)
    assemble(0, False)
    copies = exchange(0, False)
    start(copies)
    late_nodes()
    arrive(copies[6:])
    before_x(0, False)
    arrive(copies[:6])
    after_x(0)

    def substep(s, carry):
        forces(s)
        assemble(s, False)
        copies = exchange(s, False)
        start(copies)
        arrive(copies[6:])
        before_x(s, False)
        arrive(copies[:6])
        after_x(s)
        return carry

    lax.fori_loop(1, SUBSTEPS - 1, substep, 0)
    s = SUBSTEPS - 1
    forces(s)
    assemble(s, True)
    copies = exchange(s, True)
    start(copies)
    arrive(copies[2:])
    before_x(s, True)

    rows = []
    for source in (u_all, v_own):
        for c in range(3):
            for j in range(4):
                rows.append(jnp.concatenate([source[c, group(k * 4 + j), :] for k in range(4)], axis=1))
    result = permute(jnp.concatenate(rows, axis=0), gather_vm[...])
    for a, target in enumerate((uo_vm, vo_vm)):
        for c in range(3):
            for j in range(4):
                row = ((a * 3 + c) * 4 + j) * 8
                for b in range(4):
                    target[c, pl.ds(4 * b + j, 4, stride=16), :] = result[row : row + 4, b * 128 : (b + 1) * 128]

    arrive(copies[:2])
    with_corner(s, XF, DPP)
    scale = im_own[pl.ds(0, 16, stride=8), :]
    for c in range(3):
        change = scale * recv_x[s, XF, c * 16 : c * 16 + 16, :]
        for k in range(4):
            x_face[k, c * 4 : c * 4 + 4, :] = change[4 * k : 4 * k + 4]
    result = permute(wide(x_face, 0, 16), gather_vm[...])
    for c in range(3):
        for b in range(4):
            rows = slice(4 * b, 4 * b + 4)
            value = result[c * 4 : c * 4 + 4, b * 128 : (b + 1) * 128]
            vo_vm[c, rows, :] = vo_vm[c, rows, :] - value
            uo_vm[c, rows, :] = uo_vm[c, rows, :] - TIME_STEP * value
    for copy, to in zip(halos, halo_to):

        @pl.when(present(*to))
        def _():
            copy.wait_send()

    def drain(s, carry):
        finish(exchange(s, False))
        return carry

    lax.fori_loop(0, SUBSTEPS - 1, drain, 0)
    finish(exchange(SUBSTEPS - 1, True))


def write_out(u_ref, v_ref, uo_ref, vo_ref, sem):
    copies = [
        pltpu.make_async_copy(u_ref, uo_ref, sem.at[0]),
        pltpu.make_async_copy(v_ref, vo_ref, sem.at[1]),
    ]
    for copy in copies:
        copy.start()
    for copy in copies:
        copy.wait()


def shards(nx, ny, displacement, velocity, inverse_mass, lame_first, lame_second, level_map):
    spread, gather, pack = (jnp.asarray(table) for table in tables())
    vmem = pltpu.VMEM
    uo, vo = pl.pallas_call(
        functools.partial(kernel, nx, ny),
        out_shape=[jax.ShapeDtypeStruct((3, 64, 128), F32)] * 2,
        in_specs=[pl.BlockSpec(memory_space=pltpu.HBM)] * 9,
        out_specs=[pl.BlockSpec(memory_space=pltpu.VMEM)] * 2,
        scratch_shapes=[
            vmem((3, 64, 128), F32),
            vmem((4, 64, 128), F32),
            vmem((5, 5, 5, 1, 128), F32),
            vmem((5, 5, 5, 1, 128), F32),
            vmem((200, 128), F32),
            vmem((200, 128), F32),
            vmem((200, 128), F32),
            vmem((1, 128), jnp.int32),
            vmem((512, 512), BF16),
            vmem((512, 512), BF16),
            vmem((128, 128), BF16),
            vmem((3, 16, 128), F32),
            vmem((4, 16, 128), F32),
            vmem((32, 128), F32),
            vmem((32, 128), F32),
            vmem((8, 128), F32),
            vmem((8, 128), F32),
            vmem((4, 224, 128), F32),
            vmem((4, 16, 128), F32),
            vmem((56, 128), F32),
            vmem((3, 200, 128), F32),
            vmem((3, 128, 128), F32),
            vmem((128, 128), F32),
            vmem((24, 128), F32),
            vmem((24, 128), F32),
            vmem((8, 128), F32),
            vmem((3, 200, 128), F32),
            vmem((3, 200, 128), F32),
            vmem((3, 200, 128), F32),
            vmem((3, 200, 128), F32),
            vmem((3, 128, 128), F32),
            vmem((24, 128), F32),
            vmem((24, 128), F32),
            vmem((SUBSTEPS, 2, 56, 128), F32),
            vmem((SUBSTEPS, 4, 8, 128), F32),
            vmem((SUBSTEPS, 2, 24, 128), F32),
            vmem((SUBSTEPS, 2, 56, 128), F32),
            vmem((SUBSTEPS, 4, 8, 128), F32),
            vmem((SUBSTEPS, 2, 24, 128), F32),
            pltpu.SemaphoreType.DMA((9,)),
            pltpu.SemaphoreType.DMA((5,)),
            pltpu.SemaphoreType.DMA((5,)),
            pltpu.SemaphoreType.DMA((SUBSTEPS, 8)),
            pltpu.SemaphoreType.DMA((SUBSTEPS, 8)),
        ],
        compiler_params=pltpu.CompilerParams(collective_id=0, has_side_effects=True, vmem_limit_bytes=16 * 2**20),
        name="substeps",
    )(
        *(
            pltpu.with_memory_space_constraint(array, pltpu.HBM)
            for array in (
                displacement.reshape(3, 64, 128),
                velocity.reshape(3, 64, 128),
                inverse_mass.reshape(1, 64, 128),
                lame_first,
                lame_second,
                level_map,
                spread,
                gather,
                pack,
            )
        )
    )
    uo, vo = pl.pallas_call(
        write_out,
        out_shape=[jax.ShapeDtypeStruct((3, 64, 128), F32)] * 2,
        in_specs=[pl.BlockSpec(memory_space=pl.ANY)] * 2,
        out_specs=[pl.BlockSpec(memory_space=pl.ANY)] * 2,
        scratch_shapes=[pltpu.SemaphoreType.DMA((2,))],
        compiler_params=pltpu.CompilerParams(vmem_limit_bytes=2**20),
        name="write_out",
    )(uo, vo)
    return uo.reshape(3, 4, 16, 128), vo.reshape(3, 4, 16, 128)


def solution(mesh):
    in_specs = (
        P(None, "px", "py", None),
        P(None, "px", "py", None),
        P("px", "py", None),
        P(None, None, None, "px", "py"),
        P(None, None, None, "px", "py"),
        P("px", "py"),
    )
    out_specs = (P(None, "px", "py", None), P(None, "px", "py", None))
    body = functools.partial(shards, mesh.shape["px"], mesh.shape["py"])
    return jax.shard_map(body, mesh=mesh, in_specs=in_specs, out_specs=out_specs, check_vma=False)
```

```python
import functools

import jax
import jax.numpy as jnp
import ml_dtypes
import numpy as np
from jax import lax
from jax.experimental import pallas as pl
from jax.experimental.pallas import tpu as pltpu
from jax.sharding import PartitionSpec as P

SUBSTEPS = 4
TIME_STEP = 0.1
MESH = pl.DeviceIdType.MESH
F32 = jnp.float32
BF16 = jnp.bfloat16
NEIGHBOURS = [(1, 0), (-1, 0), (1, 1), (1, -1), (-1, 1), (-1, -1), (0, 1), (0, -1)]
SLOT = {d: n for n, d in enumerate(NEIGHBOURS)}
XF, XB, DPP, DPM, DMP, DMM, YU, YD = range(8)


def gll_tables():
    points = np.array([-1.0, -np.sqrt(3.0 / 7.0), 0.0, np.sqrt(3.0 / 7.0), 1.0])
    weights = np.array([0.1, 49.0 / 90.0, 32.0 / 45.0, 49.0 / 90.0, 0.1])
    legendre = (35.0 * points**4 - 30.0 * points**2 + 3.0) / 8.0
    derivative = np.zeros((5, 5))
    for row in range(5):
        for col in range(5):
            if row != col:
                derivative[row, col] = legendre[row] / (legendre[col] * (points[row] - points[col]))
    derivative[0, 0] = -5.0
    derivative[4, 4] = 5.0
    return derivative, weights


def place(k, j):
    if k < 4 and j < 4:
        return k * 4 + j
    return 16 + k if k < 4 else 20 + j


@functools.cache
def tables():
    spread = np.zeros((512, 512), ml_dtypes.bfloat16)
    pack = np.zeros((128, 128), ml_dtypes.bfloat16)
    for k in range(4):
        for c in range(32):
            pack[4 * c + k, k * 32 + c] = 1
            for b in range(4):
                spread[b * 128 + 4 * c + k, k * 128 + b * 32 + c] = 1
    return spread, np.ascontiguousarray(spread.T), pack


def apply(matrix, v):
    even0, odd0 = v[0] + v[4], v[0] - v[4]
    even1, odd1 = v[1] + v[3], v[1] - v[3]
    out = [None] * 5
    for a in range(2):
        row = matrix[a]
        first = float(row[0] - row[4]) / 2 * odd0 + float(row[1] - row[3]) / 2 * odd1
        second = float(row[0] + row[4]) / 2 * even0 + float(row[1] + row[3]) / 2 * even1 + float(row[2]) * v[2]
        out[a], out[4 - a] = first + second, first - second
    out[2] = float(matrix[2][0]) * odd0 + float(matrix[2][1]) * odd1
    return out


def halves(value):
    high = value.astype(BF16)
    return high, (value - high.astype(F32)).astype(BF16)


def permute(value, matrix):
    high, low = halves(value)
    rows = value.shape[0]
    out = jnp.dot(jnp.concatenate([high, low], axis=0), matrix, preferred_element_type=F32)
    return out[:rows] + out[rows:]


def kernel(
    nx,
    ny,
    u_hbm,
    v_hbm,
    im_hbm,
    la_hbm,
    mu_hbm,
    level_hbm,
    spread_hbm,
    gather_hbm,
    pack_hbm,
    uo_vm,
    vo_vm,
    u_vm,
    vim_vm,
    la_raw,
    mu_raw,
    la_vm,
    mu_vm,
    mu_twice,
    level_vm,
    spread_vm,
    gather_vm,
    pack_vm,
    halo_u,
    halo_vim,
    halo_y_send,
    halo_y,
    halo_c_send,
    halo_c,
    x_own,
    x_face,
    x_line,
    u_all,
    v_own,
    im_own,
    u_line,
    v_line,
    im_line,
    grad_z,
    stress_x,
    f_new,
    f_kept,
    f_sum,
    pack_up,
    pack_down,
    send_x,
    send_d,
    send_y,
    recv_x,
    recv_d,
    recv_y,
    load_sem,
    halo_send_sem,
    halo_recv_sem,
    send_sem,
    recv_sem,
):
    px, py = lax.axis_index("px"), lax.axis_index("py")

    def present(dx, dy):
        conditions = []
        if dx:
            conditions.append(px < nx - 1 if dx > 0 else px > 0)
        if dy:
            conditions.append(py < ny - 1 if dy > 0 else py > 0)
        return functools.reduce(jnp.logical_and, conditions)

    barrier = pltpu.get_barrier_semaphore()
    for dx, dy in NEIGHBOURS:

        @pl.when(present(dx, dy))
        def _():
            pl.semaphore_signal(barrier, inc=1, device_id=(px + dx, py + dy), device_id_type=MESH)

    loads = []
    for n, (source, target) in enumerate(
        [
            (u_hbm, u_vm),
            (v_hbm, vim_vm.at[0:3]),
            (im_hbm, vim_vm.at[3:4]),
            (spread_hbm, spread_vm),
            (pack_hbm, pack_vm),
            (la_hbm, la_raw),
            (mu_hbm, mu_raw),
            (level_hbm, level_vm),
            (gather_hbm, gather_vm),
        ]
    ):
        loads.append(pltpu.make_async_copy(source, target, load_sem.at[n]))
        loads[-1].start()

    x_own[...] = jnp.zeros_like(x_own)
    x_line[...] = jnp.zeros_like(x_line)
    x_face[...] = jnp.zeros_like(x_face)
    u_all[...] = jnp.zeros_like(u_all)

    for n, (dx, dy) in enumerate(NEIGHBOURS):

        @pl.when(jnp.logical_not(present(-dx, -dy)))
        def _():
            for s in range(SUBSTEPS):
                if n < 2:
                    recv_x[s, n] = jnp.zeros_like(recv_x[s, n])
                elif n < 6:
                    recv_d[s, n - 2] = jnp.zeros_like(recv_d[s, n - 2])
                else:
                    recv_y[s, n - 6] = jnp.zeros_like(recv_y[s, n - 6])
            if n == XB:
                halo_u[...] = jnp.zeros_like(halo_u)
                halo_vim[...] = jnp.zeros_like(halo_vim)
            if n == YD:
                halo_y[...] = jnp.zeros_like(halo_y)
            if n == DMM:
                halo_c[...] = jnp.zeros_like(halo_c)

    for n in range(3):
        loads[n].wait()
    for c in range(7):
        source = u_vm.at[c] if c < 3 else vim_vm.at[c - 3]
        halo_y_send[4 * c : 4 * c + 4, :] = source[pl.ds(0, 4, stride=16), :]
        halo_c_send[c : c + 1, :] = source[0:1, :]

    def remote(source, target, sems, n, dx, dy):
        send, recv = sems
        return pltpu.make_async_remote_copy(
            src_ref=source,
            dst_ref=target,
            send_sem=send.at[n],
            recv_sem=recv.at[n],
            device_id=(px + dx, py + dy),
            device_id_type=MESH,
        )

    halo_sems = (halo_send_sem, halo_recv_sem)
    halos = [
        remote(u_hbm.at[:, 0:16, :], halo_u, halo_sems, 0, -1, 0),
        remote(halo_c_send, halo_c, halo_sems, 1, -1, -1),
        remote(halo_y_send, halo_y, halo_sems, 2, 0, -1),
        remote(v_hbm.at[:, 0:16, :], halo_vim.at[0:3], halo_sems, 3, -1, 0),
        remote(im_hbm.at[:, 0:16, :], halo_vim.at[3:4], halo_sems, 4, -1, 0),
    ]
    halo_to = [(-1, 0), (-1, -1), (0, -1), (-1, 0), (-1, 0)]

    neighbours = 0
    for dx, dy in NEIGHBOURS:
        neighbours = neighbours + present(dx, dy).astype(jnp.int32)
    pl.semaphore_wait(barrier, neighbours)
    for copy, to in zip(halos, halo_to):

        @pl.when(present(*to))
        def _():
            copy.start()

    def wait_halo(n):
        dx, dy = halo_to[n]

        @pl.when(present(-dx, -dy))
        def _():
            halos[n].wait_recv()

    lane = lax.broadcasted_iota(jnp.int32, (8, 128), 1)
    sublane = lax.broadcasted_iota(jnp.int32, (8, 128), 0)
    depth = lane & 31
    column = lane >> 5

    def fill_own(c, source):
        for j in range(4):
            for b in range(4):
                row = (c * 4 + j) * 8
                x_own[b, row : row + 4, :] = source[pl.ds(4 * b + j, 4, stride=16), :]

    def wide(ref, first_row, rows):
        return jnp.concatenate([ref[b, first_row : first_row + rows, :] for b in range(4)], axis=1)

    def far_rows(source, count):
        for c in range(count):
            for b in range(4):
                x_face[b, c * 4 : c * 4 + 4, :] = source[c, 4 * b : 4 * b + 4, :]
        return permute(wide(x_face, 0, 16), spread_vm[...])

    for c in range(3):
        fill_own(c, u_vm.at[c])
    for c in range(4):
        fill_own(3 + c, vim_vm.at[c])
    loads[3].wait()
    loads[4].wait()
    for n in range(5, 9):
        loads[n].wait()
    derivative, weights = gll_tables()
    la_vm[...] = jnp.zeros_like(la_vm)
    mu_vm[...] = jnp.zeros_like(mu_vm)
    for k in range(5):
        for j in range(5):
            for i in range(5):
                weight = float(weights[i] * weights[j] * weights[k])
                row = (k * 5 + j) * 8 + i
                la_vm[row : row + 1, :] = weight * la_raw[i, j, k]
                mu_vm[row : row + 1, :] = weight * mu_raw[i, j, k]
    mu_twice[...] = 2.0 * mu_vm[...]

    nodes = permute(wide(x_own, 0, 224), spread_vm[...])
    for c in range(7):
        for j in range(4):
            for k in range(4):
                row = (c * 4 + j) * 8
                rows = pl.ds((k * 4 + j) * 8, 8)
                value = nodes[row : row + 8, k * 128 : (k + 1) * 128]
                if c < 3:
                    u_all[c, rows, :] = value
                elif c < 6:
                    v_own[c - 3, rows, :] = value
                else:
                    im_own[rows, :] = TIME_STEP * value

    wait_halo(2)
    for c in range(7):
        x_line[c * 8 : c * 8 + 4, :] = halo_y[4 * c : 4 * c + 4, :]
    wait_halo(0)
    wait_halo(1)
    face = far_rows(halo_u, 3)
    for c in range(3):
        for k in range(4):
            u_all[c, pl.ds(k * 32 + 4, 4, stride=8), :] = face[c * 4 : c * 4 + 4, k * 128 : (k + 1) * 128]
    for c in range(7):
        x_line[c * 8 + 4 : c * 8 + 5, :] = halo_c[c : c + 1, :]
    u_line[...] = permute(x_line[0:24, :], pack_vm[...])

    def group(p):
        return pl.ds(p * 8, 8)

    def expand():
        for c in range(3):
            line = u_line[c * 8 : c * 8 + 8, :]
            for k in range(4):
                inner = pltpu.roll(u_all[c, group(k * 4), :], 96, 1)
                outer = pltpu.roll(line, (96 - 32 * k) % 128, 1) if k != 3 else line
                u_all[c, group(16 + k), :] = jnp.where(column == 3, outer, inner)
            for j in range(5):
                below = pltpu.roll(u_all[c, group(j if j < 4 else 16), :], 127, 1)
                u_all[c, group(20 + j), :] = jnp.where(depth < 31, below, 0.0)

    def columns(matrix):
        out = []
        for n in range(5):
            values = jnp.zeros((8, 128), F32)
            for i in range(5):
                values = jnp.where(sublane == i, float(matrix[i][n]), values)
            out.append(values)
        return out

    def along_x(vectors, ref, c, row):
        total = vectors[0] * jnp.broadcast_to(ref[c, row : row + 1, :], (8, 128))
        for n in range(1, 5):
            total = total + vectors[n] * jnp.broadcast_to(ref[c, row + n : row + n + 1, :], (8, 128))
        return total

    def forces(s):
        forward, backward = columns(derivative), columns(derivative.T)
        for c in range(3):
            for j in range(5):
                out = apply(derivative, [u_all[c, group(place(k, j)), :] for k in range(5)])
                for k in range(5):
                    grad_z[c, group(k * 5 + j), :] = out[k]
        for k in range(5):
            gy = [apply(derivative, [u_all[c, group(place(k, j)), :] for j in range(5)]) for c in range(3)]
            stress_y = [[], [], []]
            for j in range(5):
                rows = group(k * 5 + j)
                gx = [along_x(forward, u_all, c, place(k, j) * 8) for c in range(3)]
                gz = [grad_z[c, rows, :] for c in range(3)]
                first, second, twice = la_vm[rows, :], mu_vm[rows, :], mu_twice[rows, :]
                pressure = first * (gx[0] + gy[1][j] + gz[2])
                xy = second * (gy[0][j] + gx[1])
                xz = second * (gz[0] + gx[2])
                yz = second * (gz[1] + gy[2][j])
                stress_x[0, rows, :] = pressure + twice * gx[0]
                stress_x[1, rows, :] = xy
                stress_x[2, rows, :] = xz
                stress_y[0].append(xy)
                stress_y[1].append(pressure + twice * gy[1][j])
                stress_y[2].append(yz)
                grad_z[0, rows, :] = xz
                grad_z[1, rows, :] = yz
                grad_z[2, rows, :] = pressure + twice * gz[2]
            for c in range(3):
                out = apply(derivative.T, stress_y[c])
                for j in range(5):
                    f_new[c, group(k * 5 + j), :] = out[j] + along_x(backward, stress_x, c, (k * 5 + j) * 8)
        least = jnp.where(s == 0, 0, jnp.where(s == 2, 1, 2))
        active = jnp.broadcast_to(level_vm[...], (8, 128)) >= least
        for c in range(3):
            for j in range(5):
                out = apply(derivative.T, [grad_z[c, group(k * 5 + j), :] for k in range(5)])
                for k in range(5):
                    new = f_new[c, group(k * 5 + j), :] + out[k]
                    rows = group(place(k, j))
                    f_kept[c, rows, :] = jnp.where(active, new, f_kept[c, rows, :])

    def assemble(s, last):
        for c in range(3):
            f = [f_kept[c, group(p), :] for p in range(25)]
            for j in range(5):
                p = j if j < 4 else 16
                f[p] = f[p] + jnp.where(depth > 0, pltpu.roll(f[20 + j], 1, 1), 0.0)
            up = jnp.zeros((8, 128), F32)
            down = jnp.zeros((8, 128), F32)
            for k in range(4):
                shifted = pltpu.roll(f[16 + k], 32, 1)
                up = jnp.where(column == k, pltpu.roll(shifted, 32 * k, 1) if k else shifted, up)
                down = jnp.where(column == k, pltpu.roll(f[4 * k], 32 * k, 1) if k else f[0], down)
                f[4 * k] = f[4 * k] + jnp.where(column > 0, shifted, 0.0)
            for p in range(16):
                f_sum[c, group(p), :] = f[p]
            pack_up[c * 8 : c * 8 + 8, :] = up
            pack_down[c * 8 : c * 8 + 8, :] = down
        for c in range(3):
            send_x[s, XF, c * 16 : c * 16 + 16, :] = f_sum[c, pl.ds(4, 16, stride=8), :]
            if not last:
                send_x[s, XB, c * 16 : c * 16 + 16, :] = f_sum[c, pl.ds(0, 16, stride=8), :]
        up_far = pack_up[pl.ds(4, 3, stride=8), :]
        send_d[s, DPP - 2, 0:3, :] = up_far
        send_y[s, 0] = pack_up[...]
        if not last:
            up_near = pack_up[pl.ds(0, 3, stride=8), :]
            send_d[s, DPM - 2, 0:3, :] = pack_down[pl.ds(4, 3, stride=8), :]
            send_d[s, DMP - 2, 0:3, :] = up_near
            send_d[s, DMM - 2, 0:3, :] = pack_down[pl.ds(0, 3, stride=8), :]
            send_x[s, XF, 48:51, :] = up_far
            send_x[s, XB, 48:51, :] = up_near
            send_y[s, 1] = pack_down[...]

    def exchange(s, last):
        copies = []
        for n, (dx, dy) in enumerate(NEIGHBOURS):
            if last and (dx < 0 or dy < 0):
                continue
            if n < 2:
                pair = (send_x.at[s, n], recv_x.at[s, n])
            elif n < 6:
                pair = (send_d.at[s, n - 2], recv_d.at[s, n - 2])
            else:
                pair = (send_y.at[s, n - 6], recv_y.at[s, n - 6])
            copies.append(((dx, dy), remote(*pair, (send_sem.at[s], recv_sem.at[s]), n, dx, dy)))
        return copies

    def start(copies):
        for to, copy in copies:

            @pl.when(present(*to))
            def _():
                copy.start()

    def arrive(copies):
        for (dx, dy), copy in copies:

            @pl.when(present(-dx, -dy))
            def _():
                copy.wait_recv()

    def finish(copies):
        for to, copy in copies:

            @pl.when(present(*to))
            def _():
                copy.wait_send()

    def before_x(s, last):
        for c in range(3):
            rows = slice(c * 8, c * 8 + 8)
            near = recv_y[s, 0, rows, :]
            for k in range(4):
                part = pltpu.roll(near, 128 - 32 * k, 1) if k else near
                f_sum[c, group(4 * k), :] = f_sum[c, group(4 * k), :] + jnp.where(column == 0, part, 0.0)
            v = v_own[c] - im_own[...] * f_sum[c]
            v_own[c] = v
            u_all[c, 0:128, :] = u_all[c, 0:128, :] + TIME_STEP * v
            if not last:
                v = v_line[rows, :] - im_line[...] * (pack_up[rows, :] + recv_y[s, 1, rows, :])
                v_line[rows, :] = v
                u_line[rows, :] = u_line[rows, :] + TIME_STEP * v

    def with_corner(s, n, corner):
        for k in range(4):
            value = recv_d[s, corner - 2]
            part = pltpu.roll(value, 128 - 32 * k, 1) if k else value
            rows = pl.ds(4 * k, 3, stride=16)
            recv_x[s, n, rows, :] = recv_x[s, n, rows, :] + jnp.where(column == 0, part, 0.0)[0:3]

    def after_x(s):
        for n, corner, i in ((XF, DPP, 0), (XB, DMP, 4)):
            with_corner(s, n, corner)
            rows = pl.ds(i, 16, stride=8)
            scale = im_own[rows, :]
            for c in range(3):
                change = scale * recv_x[s, n, c * 16 : c * 16 + 16, :]
                v_own[c, rows, :] = v_own[c, rows, :] - change
                u_all[c, rows, :] = u_all[c, rows, :] - TIME_STEP * change
        for c in range(3):
            rows = slice(c * 8, c * 8 + 8)
            left = recv_x[s, XF, 48 + c : 49 + c, :] + recv_d[s, DPM - 2, c : c + 1, :]
            right = recv_x[s, XB, 48 + c : 49 + c, :] + recv_d[s, DMM - 2, c : c + 1, :]
            far = jnp.where(sublane == 0, left, jnp.where(sublane == 4, right, 0.0))
            change = im_line[...] * far
            v_line[rows, :] = v_line[rows, :] - change
            u_line[rows, :] = u_line[rows, :] - TIME_STEP * change
        expand()

    def late_nodes():
        v_line[...] = permute(x_line[24:48, :], pack_vm[...])
        im_line[...] = TIME_STEP * permute(x_line[48:56, :], pack_vm[...])
        wait_halo(3)
        wait_halo(4)
        face = far_rows(halo_vim, 4)
        for c in range(4):
            for k in range(4):
                rows = pl.ds(k * 32 + 4, 4, stride=8)
                value = face[c * 4 : c * 4 + 4, k * 128 : (k + 1) * 128]
                if c < 3:
                    v_own[c, rows, :] = value
                else:
                    im_own[rows, :] = TIME_STEP * value

    expand()
    forces(0)
    assemble(0, False)
    copies = exchange(0, False)
    start(copies)
    late_nodes()
    arrive(copies[6:])
    before_x(0, False)
    arrive(copies[:6])
    after_x(0)

    def substep(s, carry):
        forces(s)
        assemble(s, False)
        copies = exchange(s, False)
        start(copies)
        arrive(copies[6:])
        before_x(s, False)
        arrive(copies[:6])
        after_x(s)
        return carry

    lax.fori_loop(1, SUBSTEPS - 1, substep, 0)
    s = SUBSTEPS - 1
    forces(s)
    assemble(s, True)
    copies = exchange(s, True)
    start(copies)
    arrive(copies[2:])
    before_x(s, True)

    rows = []
    for source in (u_all, v_own):
        for c in range(3):
            for j in range(4):
                rows.append(jnp.concatenate([source[c, group(k * 4 + j), :] for k in range(4)], axis=1))
    result = permute(jnp.concatenate(rows, axis=0), gather_vm[...])
    for a, target in enumerate((uo_vm, vo_vm)):
        for c in range(3):
            for j in range(4):
                row = ((a * 3 + c) * 4 + j) * 8
                for b in range(4):
                    target[c, pl.ds(4 * b + j, 4, stride=16), :] = result[row : row + 4, b * 128 : (b + 1) * 128]

    for copy, to in zip(halos, halo_to):

        @pl.when(present(*to))
        def _():
            copy.wait_send()

    def drain(s, carry):
        finish(exchange(s, False))
        return carry

    lax.fori_loop(0, SUBSTEPS - 1, drain, 0)

    arrive(copies[:2])
    with_corner(s, XF, DPP)
    scale = im_own[pl.ds(0, 16, stride=8), :]
    for c in range(3):
        change = scale * recv_x[s, XF, c * 16 : c * 16 + 16, :]
        for k in range(4):
            x_face[k, c * 4 : c * 4 + 4, :] = change[4 * k : 4 * k + 4]
    result = permute(wide(x_face, 0, 16), gather_vm[...])
    for c in range(3):
        for b in range(4):
            rows = slice(4 * b, 4 * b + 4)
            value = result[c * 4 : c * 4 + 4, b * 128 : (b + 1) * 128]
            vo_vm[c, rows, :] = vo_vm[c, rows, :] - value
            uo_vm[c, rows, :] = uo_vm[c, rows, :] - TIME_STEP * value
    finish(exchange(SUBSTEPS - 1, True))


def write_out(u_ref, v_ref, uo_ref, vo_ref, sem):
    copies = [
        pltpu.make_async_copy(u_ref, uo_ref, sem.at[0]),
        pltpu.make_async_copy(v_ref, vo_ref, sem.at[1]),
    ]
    for copy in copies:
        copy.start()
    for copy in copies:
        copy.wait()


def shards(nx, ny, displacement, velocity, inverse_mass, lame_first, lame_second, level_map):
    spread, gather, pack = (jnp.asarray(table) for table in tables())
    vmem = pltpu.VMEM
    uo, vo = pl.pallas_call(
        functools.partial(kernel, nx, ny),
        out_shape=[jax.ShapeDtypeStruct((3, 64, 128), F32)] * 2,
        in_specs=[pl.BlockSpec(memory_space=pltpu.HBM)] * 9,
        out_specs=[pl.BlockSpec(memory_space=pltpu.VMEM)] * 2,
        scratch_shapes=[
            vmem((3, 64, 128), F32),
            vmem((4, 64, 128), F32),
            vmem((5, 5, 5, 1, 128), F32),
            vmem((5, 5, 5, 1, 128), F32),
            vmem((200, 128), F32),
            vmem((200, 128), F32),
            vmem((200, 128), F32),
            vmem((1, 128), jnp.int32),
            vmem((512, 512), BF16),
            vmem((512, 512), BF16),
            vmem((128, 128), BF16),
            vmem((3, 16, 128), F32),
            vmem((4, 16, 128), F32),
            vmem((32, 128), F32),
            vmem((32, 128), F32),
            vmem((8, 128), F32),
            vmem((8, 128), F32),
            vmem((4, 224, 128), F32),
            vmem((4, 16, 128), F32),
            vmem((56, 128), F32),
            vmem((3, 200, 128), F32),
            vmem((3, 128, 128), F32),
            vmem((128, 128), F32),
            vmem((24, 128), F32),
            vmem((24, 128), F32),
            vmem((8, 128), F32),
            vmem((3, 200, 128), F32),
            vmem((3, 200, 128), F32),
            vmem((3, 200, 128), F32),
            vmem((3, 200, 128), F32),
            vmem((3, 128, 128), F32),
            vmem((24, 128), F32),
            vmem((24, 128), F32),
            vmem((SUBSTEPS, 2, 56, 128), F32),
            vmem((SUBSTEPS, 4, 8, 128), F32),
            vmem((SUBSTEPS, 2, 24, 128), F32),
            vmem((SUBSTEPS, 2, 56, 128), F32),
            vmem((SUBSTEPS, 4, 8, 128), F32),
            vmem((SUBSTEPS, 2, 24, 128), F32),
            pltpu.SemaphoreType.DMA((9,)),
            pltpu.SemaphoreType.DMA((5,)),
            pltpu.SemaphoreType.DMA((5,)),
            pltpu.SemaphoreType.DMA((SUBSTEPS, 8)),
            pltpu.SemaphoreType.DMA((SUBSTEPS, 8)),
        ],
        compiler_params=pltpu.CompilerParams(collective_id=0, has_side_effects=True, vmem_limit_bytes=16 * 2**20),
        name="substeps",
    )(
        *(
            pltpu.with_memory_space_constraint(array, pltpu.HBM)
            for array in (
                displacement.reshape(3, 64, 128),
                velocity.reshape(3, 64, 128),
                inverse_mass.reshape(1, 64, 128),
                lame_first,
                lame_second,
                level_map,
                spread,
                gather,
                pack,
            )
        )
    )
    uo, vo = pl.pallas_call(
        write_out,
        out_shape=[jax.ShapeDtypeStruct((3, 64, 128), F32)] * 2,
        in_specs=[pl.BlockSpec(memory_space=pl.ANY)] * 2,
        out_specs=[pl.BlockSpec(memory_space=pl.ANY)] * 2,
        scratch_shapes=[pltpu.SemaphoreType.DMA((2,))],
        compiler_params=pltpu.CompilerParams(vmem_limit_bytes=2**20),
        name="write_out",
    )(uo, vo)
    return uo.reshape(3, 4, 16, 128), vo.reshape(3, 4, 16, 128)


def solution(mesh):
    in_specs = (
        P(None, "px", "py", None),
        P(None, "px", "py", None),
        P("px", "py", None),
        P(None, None, None, "px", "py"),
        P(None, None, None, "px", "py"),
        P("px", "py"),
    )
    out_specs = (P(None, "px", "py", None), P(None, "px", "py", None))
    body = functools.partial(shards, mesh.shape["px"], mesh.shape["py"])
    return jax.shard_map(body, mesh=mesh, in_specs=in_specs, out_specs=out_specs, check_vma=False)
```
